256 devices in a mesh: row: 16 (over z, core), col: 8 (over y, x_hi), pair: 2 (over x_lo).
Axes of the slice: x: 4 (x_hi: 2, x_lo: 2; x = x_hi * 2 + x_lo), y: 4, z: 8, core: 2. Of those that a mesh axis runs over, the one named last changes fastest.
Arguments:
- amplitudes: bfloat16 [320, 8, 320], P('row', 'pair', 'col'), may hold values from -6 to 6
- factors: bfloat16 [2048, 320, 320], P(('row', 'col', 'pair')), may hold values from -0.125 to 0.125
- vir_irrep: int32 [320], replicated, may hold values from 0 to 7, never falling along the last dimension, each value on 1 to 80 neighbouring positions
- pair_irrep: int32 [8], P('pair'), may hold values from 0 to 7
Outputs:
- ladder_term: float32 [320, 8, 320], P('row', 'pair', 'col')
The draws below stay inside these ranges and needn't reach their ends.
Inputs may be any that keep to these rules, and one draw needn't show every extreme that they name: `vir_irrep`: labels never fall along the virtual index, so each label holds one contiguous block of virtuals.
All inputs are finite; a program needn't handle non-finite values.
Results may differ from the reference program's by a relative error of at most 0.0025.
Values may be sent and summed in bfloat16 or wider, within the bound.
No kernel may reach another device: no remote copies, remote signals or barrier semaphores. Data moves between devices by JAX's collectives and lax.ppermute only.
A program may use at most 64 MiB of HBM per device.

```python
import math
import jax
import jax.numpy as jnp
import numpy as np
from jax import lax

V = 320
NQ = 2048
PAIRS = 8


def touch_ends(result, rng, low, largest):
    place = [jax.random.randint(jax.random.fold_in(rng, axis), (), 0, length) for axis, length in enumerate(result.shape)]
    main_axis = result.shape.index(max(result.shape))
    beside = place[:main_axis] + [(place[main_axis] + 1) % result.shape[main_axis]] + place[main_axis + 1:]
    return result.at[tuple(place)].set(low).at[tuple(beside)].set(largest)


def raised(array, own_key, source, target, parts, factor):
    owner, partner = [(jnp.arange(array.shape[axis_at]) // (array.shape[axis_at] // parts)).reshape([-1 if axis == axis_at else 1 for axis in range(array.ndim)]) for axis_at in (source, target)]
    chosen = jax.random.permutation(own_key, parts)[partner]
    strong = (owner == chosen) | (owner == (partner + parts // 2) % parts)
    return jnp.where(strong, factor * array, array)


def block_scale(rng, shape, shards, low, largest):
    def one(dim, parts):
        steps = jax.random.uniform(jax.random.fold_in(jax.random.fold_in(rng, 6), dim), (parts,), jnp.float32, low / len(shards), largest / len(shards))
        return jnp.repeat(jnp.exp(steps), shape[dim] // parts).reshape((-1,) + (1,) * (len(shape) - dim - 1))

    level = one(*shards[0])
    for cut in shards[1:]:
        level = level * one(*cut)
    return level


def length_profile(count, total, limit, skew):
    weights = [(1 << 20) // math.isqrt(standing ** skew) + 1 for standing in range(2, count + 1)]
    surplus, given = total - limit - (count - 1), [1] * (count - 1)
    while surplus > 0:
        movable = [i for i in range(count - 1) if given[i] < limit]
        pool, remaining = sum([weights[i] for i in movable]), surplus
        for i in movable:
            addition = min(limit - given[i], max(1, remaining * weights[i] // pool), surplus)
            given[i] = given[i] + addition
            surplus = surplus - addition
    return np.array([limit] + given)


def ragged_sizes(key, amount, total, limit, skew):
    if amount == 2:
        one = jax.random.randint(key, (), max(1, total - limit), min(limit, total - 1) + 1)
        return jnp.stack([one, total - one])
    tallies = jnp.asarray(length_profile(amount, total, limit, skew), jnp.int32)
    couples = (amount - 1) // 2
    donor, taker = tallies[1:1 + 2 * couples:2], tallies[2:2 + 2 * couples:2]
    slack = jnp.minimum(donor - 1, limit - taker)
    shifted = jax.random.randint(jax.random.fold_in(key, 1), (couples,), 0, 1 << 20) % (slack + 1)
    tallies = tallies.at[1:1 + 2 * couples:2].set(donor - shifted).at[2:2 + 2 * couples:2].set(taker + shifted)
    return tallies[jax.random.permutation(jax.random.fold_in(key, 2), amount)]


def noise(rng, shape, scale, most, shards=(), dtype=jnp.bfloat16):
    loudness = block_scale(rng, shape, shards, -0.22, 0.18) if shards else 1.0
    values = jax.random.normal(rng, shape, jnp.float32) * scale * loudness
    return jnp.minimum(jnp.maximum(values, -most), most).astype(dtype)


def gaussian_with(stream_key, extent, spread, most, pieces, heavy, dtype=jnp.bfloat16):
    values = spread * jax.random.normal(stream_key, extent, jnp.float32)
    if pieces:
        values = values * block_scale(stream_key, extent, pieces, -0.22, 0.18)
    return jnp.clip(raised(values, jax.random.fold_in(stream_key, 3), *heavy), -most, most).astype(dtype)


def setup_inputs(seed: int = 0) -> dict:
    key_of = jax.random.split(jax.random.key(seed), 5)
    amplitudes = noise(key_of[0], (V, PAIRS, V), 1.0, 6.0, ((0, 16), (1, 2), (2, 8)))
    factors = gaussian_with(key_of[1], (NQ, V, V), (64 * V) ** -0.5, 0.125, ((0, 256),), (0, 1, 64, 4.0))
    vir_irrep = jnp.searchsorted(jnp.cumsum(ragged_sizes(key_of[2], 8, V, V // 4, 1)), jnp.arange(V), side="right").astype(jnp.int32)
    pair_irrep = touch_ends(jax.random.randint(key_of[3], (PAIRS,), 0, 8), jax.random.fold_in(key_of[3], 1), 0, 7).astype(jnp.int32)
    return {"amplitudes": amplitudes, "factors": factors, "vir_irrep": vir_irrep, "pair_irrep": pair_irrep}


def reference(amplitudes, factors, vir_irrep, pair_irrep):
    pair_count = amplitudes.shape[1]
    mixed = jnp.bitwise_xor(vir_irrep[:, None, None], vir_irrep[None, None, :])
    allowed = mixed == pair_irrep[None, :, None]
    sym_amp = jnp.where(allowed, amplitudes, jnp.zeros_like(amplitudes))
    amp_matrix = sym_amp.reshape(V, pair_count * V)

    def one_factor(summed, factor):
        inner = jnp.dot(factor, amp_matrix, preferred_element_type=jnp.float32).astype(jnp.bfloat16)
        inner = inner.reshape(V * pair_count, V)
        outer = jnp.dot(inner, factor.T, preferred_element_type=jnp.float32)
        return summed + outer.reshape(V, pair_count, V), None

    start = jnp.zeros((V, pair_count, V), jnp.float32)
    ladder = lax.scan(one_factor, start, factors)[0]
    both = ladder + jnp.transpose(ladder, (2, 1, 0))
    return jnp.where(allowed, both, jnp.zeros_like(both))
```

```python
import functools

import jax
import jax.numpy as jnp
from jax import lax
from jax.experimental import pallas as pl
from jax.experimental.pallas import tpu as pltpu
from jax.sharding import PartitionSpec as P

FOLD = 128


def fold_rows(x):
    total = x[:FOLD]
    for start in range(FOLD, x.shape[0], FOLD):
        piece = x[start : start + FOLD]
        total = total + jnp.pad(piece, ((0, FOLD - piece.shape[0]), (0, 0)))
    return total


def unfold_rows(x, width):
    pieces = [x[: min(FOLD, width - start)] for start in range(0, width, FOLD)]
    return jnp.concatenate(pieces, axis=0)


def both_halves(own):
    other = lax.ppermute(own, "pair", [(0, 1), (1, 0)])
    first = lax.axis_index("pair") == 0
    return jnp.concatenate([jnp.where(first, own, other), jnp.where(first, other, own)])


def ladder_kernel(
    cols, pairs_here, pair_ref, t_ref, stack_ref, side_ref, down_ref, across_ref, out_ref, inner
):
    p = pl.program_id(0)
    width = side_ref.shape[0]
    count = side_ref.shape[1] // width
    half, at = p // pairs_here, p % pairs_here
    groups = t_ref.shape[0] // cols
    want = pair_ref[p]
    allowed = jnp.bitwise_xor(down_ref[...], across_ref[...]) == want
    rows = jnp.concatenate(
        [t_ref[q * groups + half, at].astype(jnp.float32) for q in range(cols)], axis=0
    )
    tiles = -(-width // FOLD)
    spread = jnp.concatenate([rows] * tiles, axis=1)
    amp = jnp.where(allowed, spread, 0.0).astype(jnp.bfloat16)[:, :width]
    for k in range(count):
        part = lax.dot_general(
            amp,
            stack_ref[pl.ds(k * width, width), :],
            (((1,), (1,)), ((), ())),
            preferred_element_type=jnp.float32,
        )
        inner[pl.ds(k * width, width), :] = part.astype(jnp.bfloat16)
    ladder = jnp.dot(side_ref[...], inner[...], preferred_element_type=jnp.float32)
    both = ladder + ladder.T
    both = jnp.concatenate(
        [both, jnp.zeros((width, tiles * FOLD - width), jnp.float32)], axis=1
    )
    both = jnp.where(allowed, both, 0.0)
    folded = both[:, :FOLD]
    for k in range(1, tiles):
        folded = folded + both[:, k * FOLD : (k + 1) * FOLD]
    block = width // cols
    for q in range(cols):
        out_ref[q * groups + half, at] = folded[q * block : (q + 1) * block].astype(out_ref.dtype)


def ladder_call(gathered, factors, labels, pair_labels, cols, pairs_here):
    count, width, _ = factors.shape
    pairs = pair_labels.shape[0]
    tiles = -(-width // FOLD)
    stack = factors.reshape(count * width, width)
    side = jnp.transpose(factors, (1, 0, 2)).reshape(width, count * width)
    down = labels[:, None]
    across = jnp.pad(labels, (0, tiles * FOLD - width), constant_values=-1)[None, :]
    vmem = pl.BlockSpec(memory_space=pltpu.VMEM)
    return pl.pallas_call(
        functools.partial(ladder_kernel, cols, pairs_here),
        grid=(pairs,),
        out_shape=jax.ShapeDtypeStruct(gathered.shape, jnp.bfloat16),
        in_specs=[pl.BlockSpec(memory_space=pltpu.SMEM)] + [vmem] * 5,
        out_specs=vmem,
        scratch_shapes=[pltpu.VMEM((count * width, width), jnp.bfloat16)],
    )(pair_labels, gathered, stack, side, down, across)


def body(amplitudes, factors, vir_irrep, pair_irrep):
    row_block, pairs_here, col_block = amplitudes.shape
    width = vir_irrep.shape[0]
    rows, cols = width // row_block, width // col_block
    inner = pairs_here * col_block
    plane = ("col", "pair")
    row_labels = lax.dynamic_slice_in_dim(vir_irrep, lax.axis_index("row") * row_block, row_block)
    col_labels = lax.dynamic_slice_in_dim(vir_irrep, lax.axis_index("col") * col_block, col_block)
    pair_labels = both_halves(pair_irrep)
    partner = jnp.bitwise_xor(pair_irrep[:, None], col_labels[None, :]).reshape(1, inner)

    sent = jnp.broadcast_to(amplitudes.reshape(1, row_block, inner), (rows, row_block, inner))
    tall = lax.all_to_all(sent, "row", 0, 0, tiled=True).reshape(width, inner)
    tall = jnp.where(vir_irrep[:, None] == partner, tall, jnp.zeros_like(tall))
    block = fold_rows(tall).T.reshape(1, pairs_here, col_block, FOLD)
    groups = cols * lax.axis_size("pair")
    gathered = lax.all_to_all(
        jnp.broadcast_to(block, (groups, pairs_here, col_block, FOLD)), plane, 0, 0, tiled=True
    )

    partial_sums = ladder_call(gathered, factors, vir_irrep, pair_labels, cols, pairs_here)

    pieces = lax.all_to_all(partial_sums, plane, 0, 0, tiled=True)
    summed = jnp.sum(pieces.astype(jnp.float32), axis=0).reshape(inner, FOLD)
    tall_sum = unfold_rows(summed.T, width).reshape(rows, row_block, inner)
    finals = lax.all_to_all(tall_sum, "row", 0, 0, tiled=True)
    ladder = jnp.sum(finals, axis=0)
    ladder = jnp.where(row_labels[:, None] == partner, ladder, jnp.zeros_like(ladder))
    return ladder.reshape(row_block, pairs_here, col_block)


def solution(mesh):
    placed = (P("row", "pair", "col"), P(("row", "col", "pair"), None, None), P(), P("pair"))
    return jax.shard_map(
        body, mesh=mesh, in_specs=placed, out_specs=P("row", "pair", "col"), check_vma=False
    )
```

```python
import functools

import jax
import jax.numpy as jnp
from jax import lax
from jax.experimental import pallas as pl
from jax.experimental.pallas import tpu as pltpu
from jax.sharding import PartitionSpec as P

FOLD = 128
CORES = 2


def fold_rows(x):
    total = x[:FOLD]
    for start in range(FOLD, x.shape[0], FOLD):
        piece = x[start : start + FOLD]
        total = total + jnp.pad(piece, ((0, FOLD - piece.shape[0]), (0, 0)))
    return total


def unfold_rows(x, width):
    pieces = [x[: min(FOLD, width - start)] for start in range(0, width, FOLD)]
    return jnp.concatenate(pieces, axis=0)


def ladder_kernel(
    cols,
    factor_group,
    lane_group,
    pair_ref,
    t_ref,
    own_ref,
    other_ref,
    own_side_ref,
    other_side_ref,
    down_ref,
    across_ref,
    out_ref,
    inner,
    amp,
    ladders,
):
    width = own_side_ref.shape[0]
    half_depth = own_ref.shape[0]
    count = half_depth // width
    groups, pairs_here = t_ref.shape[0] // cols, t_ref.shape[1]
    pairs = groups * pairs_here
    tiles = -(-width // FOLD)
    block = width // cols
    mixed = jnp.bitwise_xor(down_ref[...], across_ref[...])

    for p in range(pairs):
        half, at = p // pairs_here, p % pairs_here
        rows = jnp.concatenate(
            [t_ref[q * groups + half, at].astype(jnp.float32) for q in range(cols)], axis=0
        )
        spread = jnp.where(mixed == pair_ref[p], jnp.concatenate([rows] * tiles, axis=1), 0.0)
        amp[p * width : (p + 1) * width, :] = spread.astype(jnp.bfloat16)[:, :width]

    step = factor_group * width
    for source, base in ((own_ref, 0), (other_ref, half_depth)):

        @pl.loop(0, count // factor_group)
        def _(g, source=source, base=base):
            part = lax.dot_general(
                amp[...],
                source[pl.ds(pl.multiple_of(g * step, step), step), :],
                (((1,), (1,)), ((), ())),
                preferred_element_type=jnp.float32,
            ).astype(jnp.bfloat16)
            for p in range(pairs):
                for k in range(factor_group):
                    at = pl.multiple_of(base + g * step + k * width, width)
                    inner[pl.ds(at, width), p * width : (p + 1) * width] = part[
                        p * width : (p + 1) * width, k * width : (k + 1) * width
                    ]

    for start in range(0, pairs * width, lane_group):
        lanes = slice(start, start + lane_group)
        ladders[:, lanes] = jnp.dot(
            own_side_ref[...], inner[:half_depth, lanes], preferred_element_type=jnp.float32
        ) + jnp.dot(
            other_side_ref[...], inner[half_depth:, lanes], preferred_element_type=jnp.float32
        )

    for p in range(pairs):
        half, at = p // pairs_here, p % pairs_here
        ladder = ladders[:, p * width : (p + 1) * width]
        both = ladder + ladder.T
        both = jnp.concatenate(
            [both, jnp.zeros((width, tiles * FOLD - width), jnp.float32)], axis=1
        )
        both = jnp.where(mixed == pair_ref[p], both, 0.0)
        folded = both[:, :FOLD]
        for k in range(1, tiles):
            folded = folded + both[:, k * FOLD : (k + 1) * FOLD]
        for q in range(cols):
            out_ref[q * groups + half, at] = folded[q * block : (q + 1) * block].astype(
                out_ref.dtype
            )


def side_by_side(factors):
    count, width, _ = factors.shape
    return jnp.transpose(factors, (1, 0, 2)).reshape(width, count * width)


def ladder_call(gathered, own, other, labels, pair_labels, cols):
    count, width, _ = own.shape
    pairs = pair_labels.shape[0]
    tiles = -(-width // FOLD)
    down = labels[:, None]
    across = jnp.pad(labels, (0, tiles * FOLD - width), constant_values=-1)[None, :]
    vmem = pl.BlockSpec(memory_space=pltpu.VMEM)
    return pl.pallas_call(
        functools.partial(ladder_kernel, cols, 4, 2 * FOLD),
        out_shape=jax.ShapeDtypeStruct(gathered.shape, jnp.bfloat16),
        in_specs=[pl.BlockSpec(memory_space=pltpu.SMEM)] + [vmem] * 7,
        out_specs=vmem,
        scratch_shapes=[
            pltpu.VMEM((2 * count * width, pairs * width), jnp.bfloat16),
            pltpu.VMEM((pairs * width, width), jnp.bfloat16),
            pltpu.VMEM((width, pairs * width), jnp.float32),
        ],
    )(
        pair_labels,
        gathered,
        own.reshape(count * width, width),
        other.reshape(count * width, width),
        side_by_side(own),
        side_by_side(other),
        down,
        across,
    )


def body(amplitudes, factors, vir_irrep, pair_irrep):
    row_block, pairs_here, col_block = amplitudes.shape
    width = vir_irrep.shape[0]
    rows, cols = width // row_block, width // col_block
    held = pairs_here // CORES
    inner = held * col_block
    plane = ("col", "pair")
    core = lax.axis_index("row") % CORES
    swap = [(k, k ^ 1) for k in range(rows)]

    other_factors = lax.ppermute(factors, "row", swap)
    other_pairs = lax.ppermute(pair_irrep, "pair", [(0, 1), (1, 0)])
    first = lax.axis_index("pair") == 0
    pair_labels = jnp.stack(
        [jnp.where(first, pair_irrep, other_pairs), jnp.where(first, other_pairs, pair_irrep)]
    )
    pair_labels = lax.dynamic_slice_in_dim(pair_labels, core * held, held, axis=1).reshape(-1)

    row_labels = lax.dynamic_slice_in_dim(vir_irrep, lax.axis_index("row") * row_block, row_block)
    col_labels = lax.dynamic_slice_in_dim(vir_irrep, lax.axis_index("col") * col_block, col_block)
    partner = jnp.bitwise_xor(pair_irrep[:, None], col_labels[None, :])
    partner_held = lax.dynamic_slice_in_dim(partner, core * held, held, axis=0).reshape(1, inner)

    halves = amplitudes.reshape(row_block, CORES, inner).transpose(1, 0, 2)
    sent = jnp.broadcast_to(halves[None], (rows // CORES, CORES, row_block, inner))
    sent = sent.reshape(rows, row_block, inner)
    tall = lax.all_to_all(sent, "row", 0, 0, tiled=True).reshape(width, inner)
    tall = jnp.where(vir_irrep[:, None] == partner_held, tall, jnp.zeros_like(tall))
    block = fold_rows(tall).T.reshape(1, held, col_block, FOLD)
    groups = cols * lax.axis_size("pair")
    gathered = lax.all_to_all(
        jnp.broadcast_to(block, (groups, held, col_block, FOLD)), plane, 0, 0, tiled=True
    )

    partial_sums = ladder_call(gathered, factors, other_factors, vir_irrep, pair_labels, cols)

    pieces = lax.all_to_all(partial_sums, plane, 0, 0, tiled=True)
    summed = jnp.sum(pieces.astype(jnp.float32), axis=0).reshape(inner, FOLD)
    tall_sum = unfold_rows(summed.T, width).reshape(rows, row_block, inner)
    finals = lax.all_to_all(tall_sum, "row", 0, 0, tiled=True)
    ladder = jnp.sum(finals.reshape(rows // CORES, CORES, row_block, inner), axis=0)
    ladder = ladder.transpose(1, 0, 2).reshape(row_block, pairs_here, col_block)
    allowed = row_labels[:, None, None] == partner[None]
    return jnp.where(allowed, ladder, jnp.zeros_like(ladder))


def solution(mesh):
    placed = (P("row", "pair", "col"), P(("row", "col", "pair"), None, None), P(), P("pair"))
    return jax.shard_map(
        body, mesh=mesh, in_specs=placed, out_specs=P("row", "pair", "col"), check_vma=False
    )
```

```python
import functools

import jax
import jax.numpy as jnp
from jax import lax
from jax.experimental import pallas as pl
from jax.experimental.pallas import tpu as pltpu
from jax.sharding import PartitionSpec as P


FOLD = 128
CORES = 2


def fold_rows(x):
    total = x[:FOLD]
    for start in range(FOLD, x.shape[0], FOLD):
        piece = x[start : start + FOLD]
        total = total + jnp.pad(piece, ((0, FOLD - piece.shape[0]), (0, 0)))
    return total


def unfold_rows(x, width):
    pieces = [x[: min(FOLD, width - start)] for start in range(0, width, FOLD)]
    return jnp.concatenate(pieces, axis=0)


def ladder_kernel(
    cols,
    group,
    lane_group,
    pair_ref,
    t_ref,
    own_ref,
    other_ref,
    down_ref,
    across_ref,
    out_ref,
    inner,
    amp,
    ladders,
    side,
    stack,
    arrived,
):
    width = down_ref.shape[0]
    half_depth = own_ref.shape[0]
    groups, pairs_here = t_ref.shape[0] // cols, t_ref.shape[1]
    pairs = groups * pairs_here
    tiles = -(-width // FOLD)
    block = width // cols
    step = group * width
    half_steps = half_depth // step

    fetch = pltpu.make_async_copy(other_ref, stack, arrived)
    fetch.start()
    mixed = jnp.bitwise_xor(down_ref[...], across_ref[...])
    for p in range(pairs):
        half, at = p // pairs_here, p % pairs_here
        rows = jnp.concatenate(
            [t_ref[q * groups + half, at].astype(jnp.float32) for q in range(cols)], axis=0
        )
        spread = jnp.where(mixed == pair_ref[p], jnp.concatenate([rows] * tiles, axis=1), 0.0)
        amp[p * width : (p + 1) * width, :] = spread.astype(jnp.bfloat16)[:, :width]

    for source, base in ((own_ref, 0), (stack, half_steps)):
        if base:
            fetch.wait()

        @pl.loop(0, half_steps)
        def _(g, source=source, base=base):
            here = pl.multiple_of(g * step, step)
            there = pl.multiple_of((base + g) * step, step)
            for k in range(group):
                side[base + g, :, k * width : (k + 1) * width] = source[
                    pl.ds(pl.multiple_of(here + k * width, width), width), :
                ]
            part = lax.dot_general(
                amp[...],
                source[pl.ds(here, step), :],
                (((1,), (1,)), ((), ())),
                preferred_element_type=jnp.float32,
            ).astype(jnp.bfloat16)
            for p in range(pairs):
                for k in range(group):
                    inner[
                        pl.ds(pl.multiple_of(there + k * width, width), width),
                        p * width : (p + 1) * width,
                    ] = part[p * width : (p + 1) * width, k * width : (k + 1) * width]

    for start in range(0, pairs * width, lane_group):
        lanes = slice(start, start + lane_group)
        total = None
        for g in range(2 * half_steps):
            term = jnp.dot(
                side[g], inner[g * step : (g + 1) * step, lanes], preferred_element_type=jnp.float32
            )
            total = term if total is None else total + term
        ladders[:, lanes] = total

    for p in range(pairs):
        half, at = p // pairs_here, p % pairs_here
        ladder = ladders[:, p * width : (p + 1) * width]
        both = ladder + ladder.T
        both = jnp.concatenate(
            [both, jnp.zeros((width, tiles * FOLD - width), jnp.float32)], axis=1
        )
        both = jnp.where(mixed == pair_ref[p], both, 0.0)
        folded = both[:, :FOLD]
        for k in range(1, tiles):
            folded = folded + both[:, k * FOLD : (k + 1) * FOLD]
        for q in range(cols):
            out_ref[q * groups + half, at] = folded[q * block : (q + 1) * block].astype(
                out_ref.dtype
            )


def ladder_call(gathered, own, other, labels, pair_labels, cols):
    count, width, _ = own.shape
    pairs = pair_labels.shape[0]
    tiles = -(-width // FOLD)
    group = 4
    depth, lanes = 2 * count * width, pairs * width
    down = labels[:, None]
    across = jnp.pad(labels, (0, tiles * FOLD - width), constant_values=-1)[None, :]
    vmem = pl.BlockSpec(memory_space=pltpu.VMEM)
    anywhere = pl.BlockSpec(memory_space=pl.ANY)
    close = functools.partial(pltpu.with_memory_space_constraint, memory_space=pltpu.VMEM)
    return pl.pallas_call(
        functools.partial(ladder_kernel, cols, group, 2 * FOLD),
        out_shape=jax.ShapeDtypeStruct(gathered.shape, jnp.bfloat16),
        in_specs=[pl.BlockSpec(memory_space=pltpu.SMEM), vmem, vmem, anywhere, vmem, vmem],
        out_specs=vmem,
        scratch_shapes=[
            pltpu.VMEM((depth, lanes), jnp.bfloat16),
            pltpu.VMEM((lanes, width), jnp.bfloat16),
            pltpu.VMEM((width, lanes), jnp.float32),
            pltpu.VMEM((2 * count // group, width, group * width), jnp.bfloat16),
            pltpu.VMEM((count * width, width), jnp.bfloat16),
            pltpu.SemaphoreType.DMA(()),
        ],
        compiler_params=pltpu.CompilerParams(vmem_limit_bytes=48 * 2**20),
    )(
        pair_labels,
        close(gathered),
        close(own.reshape(count * width, width)),
        other.reshape(count * width, width),
        close(down),
        close(across),
    )


def body(amplitudes, factors, vir_irrep, pair_irrep):
    row_block, pairs_here, col_block = amplitudes.shape
    width = vir_irrep.shape[0]
    rows, cols = width // row_block, width // col_block
    held = pairs_here // CORES
    inner = held * col_block
    plane = ("col", "pair")
    core = lax.axis_index("row") % CORES
    swap = [(k, k ^ 1) for k in range(rows)]

    other_factors = lax.ppermute(factors, "row", swap)
    other_pairs = lax.ppermute(pair_irrep, "pair", [(0, 1), (1, 0)])
    first = lax.axis_index("pair") == 0
    pair_labels = jnp.stack(
        [jnp.where(first, pair_irrep, other_pairs), jnp.where(first, other_pairs, pair_irrep)]
    )
    pair_labels = lax.dynamic_slice_in_dim(pair_labels, core * held, held, axis=1).reshape(-1)

    row_labels = lax.dynamic_slice_in_dim(vir_irrep, lax.axis_index("row") * row_block, row_block)
    col_labels = lax.dynamic_slice_in_dim(vir_irrep, lax.axis_index("col") * col_block, col_block)
    partner = jnp.bitwise_xor(pair_irrep[:, None], col_labels[None, :])
    partner_held = lax.dynamic_slice_in_dim(partner, core * held, held, axis=0).reshape(1, inner)

    halves = amplitudes.reshape(row_block, CORES, inner).transpose(1, 0, 2)
    sent = jnp.broadcast_to(halves[None], (rows // CORES, CORES, row_block, inner))
    sent = sent.reshape(rows, row_block, inner)
    tall = lax.all_to_all(sent, "row", 0, 0, tiled=True).reshape(width, inner)
    tall = jnp.where(vir_irrep[:, None] == partner_held, tall, jnp.zeros_like(tall))
    block = fold_rows(tall).T.reshape(1, held, col_block, FOLD)
    groups = cols * lax.axis_size("pair")
    gathered = lax.all_to_all(
        jnp.broadcast_to(block, (groups, held, col_block, FOLD)), plane, 0, 0, tiled=True
    )

    partial_sums = ladder_call(gathered, factors, other_factors, vir_irrep, pair_labels, cols)

    pieces = lax.all_to_all(partial_sums, plane, 0, 0, tiled=True)
    summed = jnp.sum(pieces.astype(jnp.float32), axis=0).reshape(inner, FOLD)
    tall_sum = unfold_rows(summed.T, width).reshape(rows, row_block, inner)
    tall_sum, row_labels = lax.optimization_barrier((tall_sum, row_labels))
    finals = lax.all_to_all(tall_sum, "row", 0, 0, tiled=True)
    ladder = jnp.sum(finals.reshape(rows // CORES, CORES, row_block, inner), axis=0)
    ladder = ladder.transpose(1, 0, 2).reshape(row_block, pairs_here, col_block)
    allowed = row_labels[:, None, None] == partner[None]
    return jnp.where(allowed, ladder, jnp.zeros_like(ladder))


def solution(mesh):
    placed = (P("row", "pair", "col"), P(("row", "col", "pair"), None, None), P(), P("pair"))
    return jax.shard_map(
        body, mesh=mesh, in_specs=placed, out_specs=P("row", "pair", "col"), check_vma=False
    )
```

```python
import functools

import jax
import jax.numpy as jnp
from jax import lax
from jax.experimental import pallas as pl
from jax.experimental.pallas import tpu as pltpu
from jax.sharding import PartitionSpec as P


FOLD = 128
CORES = 2


def fold_kernel(tall_ref, down_ref, partner_ref, out_ref):
    groups, held, col_block, _ = out_ref.shape
    tall = jnp.concatenate(
        [tall_ref[r].astype(jnp.float32) for r in range(tall_ref.shape[0])], axis=0
    )
    tall = jnp.where(down_ref[...] == partner_ref[...], tall, 0.0)
    folded = tall[:FOLD]
    for start in range(FOLD, tall.shape[0], FOLD):
        piece = tall[start : start + FOLD]
        short = FOLD - piece.shape[0]
        if short:
            piece = jnp.concatenate([piece, jnp.zeros((short, piece.shape[1]), jnp.float32)], axis=0)
        folded = folded + piece
    block = folded.T.astype(out_ref.dtype)
    for j in range(held):
        part = block[j * col_block : (j + 1) * col_block]
        for m in range(groups):
            out_ref[m, j] = part


def fold_call(tall, down, partner, shape):
    vmem = pl.BlockSpec(memory_space=pltpu.VMEM)
    close = functools.partial(pltpu.with_memory_space_constraint, memory_space=pltpu.VMEM)
    return pl.pallas_call(
        fold_kernel,
        out_shape=pltpu.VMEM(shape, tall.dtype),
        in_specs=[vmem] * 3,
        out_specs=vmem,
        compiler_params=pltpu.CompilerParams(vmem_limit_bytes=8 * 2**20),
    )(close(tall), close(down), close(partner))


def unfold_rows(x, width):
    pieces = [x[: min(FOLD, width - start)] for start in range(0, width, FOLD)]
    return jnp.concatenate(pieces, axis=0)


def ladder_kernel(
    cols,
    group,
    lane_group,
    pair_ref,
    t_ref,
    near_ref,
    far_ref,
    down_ref,
    across_ref,
    out_ref,
    inner,
    amp,
    ladders,
    side,
    stack,
    arrived,
):
    width = down_ref.shape[0]
    half_depth = near_ref.shape[0]
    groups, pairs_here = t_ref.shape[0] // cols, t_ref.shape[1]
    pairs = groups * pairs_here
    tiles = -(-width // FOLD)
    block = width // cols
    step = group * width
    half_steps = half_depth // step

    fetch = pltpu.make_async_copy(far_ref, stack, arrived)
    fetch.start()
    filler = jnp.full((1, tiles * FOLD - width), -1, jnp.int32)
    mixed = jnp.bitwise_xor(
        down_ref[...], jnp.concatenate([across_ref[...], filler], axis=1)
    )
    for p in range(pairs):
        half, at = p // pairs_here, p % pairs_here
        rows = jnp.concatenate(
            [t_ref[q * groups + half, at].astype(jnp.float32) for q in range(cols)], axis=0
        )
        spread = jnp.where(mixed == pair_ref[p : p + 1, :1], jnp.concatenate([rows] * tiles, axis=1), 0.0)
        amp[p * width : (p + 1) * width, :] = spread.astype(jnp.bfloat16)[:, :width]

    for source, base in ((near_ref, 0), (stack, half_steps)):
        if base:
            fetch.wait()

        @pl.loop(0, half_steps)
        def _(g, source=source, base=base):
            here = pl.multiple_of(g * step, step)
            there = pl.multiple_of((base + g) * step, step)
            for k in range(group):
                side[base + g, :, k * width : (k + 1) * width] = source[
                    pl.ds(pl.multiple_of(here + k * width, width), width), :
                ]
            part = lax.dot_general(
                amp[...],
                source[pl.ds(here, step), :],
                (((1,), (1,)), ((), ())),
                preferred_element_type=jnp.float32,
            ).astype(jnp.bfloat16)
            for p in range(pairs):
                for k in range(group):
                    inner[
                        pl.ds(pl.multiple_of(there + k * width, width), width),
                        p * width : (p + 1) * width,
                    ] = part[p * width : (p + 1) * width, k * width : (k + 1) * width]

    for start in range(0, pairs * width, lane_group):
        lanes = slice(start, start + lane_group)
        total = None
        for g in range(2 * half_steps):
            term = jnp.dot(
                side[g], inner[g * step : (g + 1) * step, lanes], preferred_element_type=jnp.float32
            )
            total = term if total is None else total + term
        ladders[:, lanes] = total

    for p in range(pairs):
        half, at = p // pairs_here, p % pairs_here
        ladder = ladders[:, p * width : (p + 1) * width]
        both = ladder + ladder.T
        both = jnp.concatenate(
            [both, jnp.zeros((width, tiles * FOLD - width), jnp.float32)], axis=1
        )
        both = jnp.where(mixed == pair_ref[p : p + 1, :1], both, 0.0)
        folded = both[:, :FOLD]
        for k in range(1, tiles):
            folded = folded + both[:, k * FOLD : (k + 1) * FOLD]
        for q in range(cols):
            out_ref[q * groups + half, at] = folded[q * block : (q + 1) * block].astype(
                out_ref.dtype
            )


def ladder_call(gathered, near, far, down, across, pair_labels, cols):
    count, width, _ = near.shape
    pairs = pair_labels.shape[0]
    group = 4
    depth, lanes = 2 * count * width, pairs * width
    vmem = pl.BlockSpec(memory_space=pltpu.VMEM)
    anywhere = pl.BlockSpec(memory_space=pl.ANY)
    close = functools.partial(pltpu.with_memory_space_constraint, memory_space=pltpu.VMEM)
    return pl.pallas_call(
        functools.partial(ladder_kernel, cols, group, 2 * FOLD),
        out_shape=pltpu.VMEM(gathered.shape, jnp.bfloat16),
        in_specs=[vmem, vmem, vmem, anywhere, vmem, vmem],
        out_specs=vmem,
        scratch_shapes=[
            pltpu.VMEM((depth, lanes), jnp.bfloat16),
            pltpu.VMEM((lanes, width), jnp.bfloat16),
            pltpu.VMEM((width, lanes), jnp.float32),
            pltpu.VMEM((2 * count // group, width, group * width), jnp.bfloat16),
            pltpu.VMEM((count * width, width), jnp.bfloat16),
            pltpu.SemaphoreType.DMA(()),
        ],
        compiler_params=pltpu.CompilerParams(vmem_limit_bytes=40 * 2**20),
    )(
        close(jnp.broadcast_to(pair_labels[:, None], (pairs, FOLD))),
        close(gathered),
        close(near.reshape(count * width, width)),
        pltpu.with_memory_space_constraint(far.reshape(count * width, width), pltpu.HBM),
        close(down),
        close(across),
    )


def body(amplitudes, factors, vir_irrep, pair_irrep):
    row_block, pairs_here, col_block = amplitudes.shape
    width = vir_irrep.shape[0]
    rows, cols = width // row_block, width // col_block
    held = pairs_here // CORES
    inner = held * col_block
    plane = ("col", "pair")
    core = lax.axis_index("row") % CORES
    swap = [(k, k ^ 1) for k in range(rows)]

    other_factors = lax.ppermute(factors, "row", swap)
    other_pairs = lax.ppermute(pair_irrep, "pair", [(0, 1), (1, 0)])
    first = lax.axis_index("pair") == 0
    pair_labels = jnp.stack(
        [jnp.where(first, pair_irrep, other_pairs), jnp.where(first, other_pairs, pair_irrep)]
    )
    pair_labels = lax.dynamic_slice_in_dim(pair_labels, core * held, held, axis=1).reshape(-1)

    row_labels = lax.dynamic_slice_in_dim(vir_irrep, lax.axis_index("row") * row_block, row_block)
    col_labels = lax.dynamic_slice_in_dim(vir_irrep, lax.axis_index("col") * col_block, col_block)
    pairs_held = lax.dynamic_slice_in_dim(pair_irrep, core * held, held)
    partner = jnp.bitwise_xor(pairs_held[:, None], col_labels[None, :]).reshape(1, inner)
    down, across = vir_irrep[:, None], vir_irrep[None, :]

    halves = amplitudes.reshape(row_block, CORES, inner).transpose(1, 0, 2)
    sent = jnp.broadcast_to(halves[None], (rows // CORES, CORES, row_block, inner))
    sent = sent.reshape(rows, row_block, inner)
    tall = lax.all_to_all(sent, "row", 0, 0, tiled=True)
    groups = cols * lax.axis_size("pair")
    block = fold_call(tall, down, partner, (groups, held, col_block, FOLD))
    gathered = lax.all_to_all(block, plane, 0, 0, tiled=True)

    partial_sums = ladder_call(gathered, other_factors, factors, down, across, pair_labels, cols)

    pieces = lax.all_to_all(partial_sums, plane, 0, 0, tiled=True)
    summed = jnp.sum(pieces.astype(jnp.float32), axis=0).reshape(inner, FOLD)
    tall_sum = unfold_rows(summed.T, width).reshape(rows, row_block, inner)
    mixed = jnp.bitwise_xor(row_labels[:, None, None], col_labels[None, None, :])
    allowed = mixed == pair_irrep[None, :, None]
    tall_sum, allowed = lax.optimization_barrier((tall_sum, allowed))
    finals = lax.all_to_all(tall_sum, "row", 0, 0, tiled=True)
    ladder = jnp.sum(finals.reshape(rows // CORES, CORES, row_block, inner), axis=0)
    ladder = ladder.transpose(1, 0, 2).reshape(row_block, pairs_here, col_block)
    return jnp.where(allowed, ladder, jnp.zeros_like(ladder))


def solution(mesh):
    placed = (P("row", "pair", "col"), P(("row", "col", "pair"), None, None), P(), P("pair"))
    return jax.shard_map(
        body, mesh=mesh, in_specs=placed, out_specs=P("row", "pair", "col"), check_vma=False
    )
```

```python
import functools

import jax
import jax.numpy as jnp
from jax import lax
from jax.experimental import pallas as pl
from jax.experimental.pallas import tpu as pltpu
from jax.sharding import PartitionSpec as P


FOLD = 128
CORES = 2


def fold_kernel(tall_ref, down_ref, partner_ref, out_ref):
    groups, held, col_block, _ = out_ref.shape
    tall = jnp.concatenate(
        [tall_ref[r].astype(jnp.float32) for r in range(tall_ref.shape[0])], axis=0
    )
    tall = jnp.where(down_ref[...] == partner_ref[...], tall, 0.0)
    folded = tall[:FOLD]
    for start in range(FOLD, tall.shape[0], FOLD):
        piece = tall[start : start + FOLD]
        short = FOLD - piece.shape[0]
        if short:
            piece = jnp.concatenate([piece, jnp.zeros((short, piece.shape[1]), jnp.float32)], axis=0)
        folded = folded + piece
    block = folded.T.astype(out_ref.dtype)
    for j in range(held):
        part = block[j * col_block : (j + 1) * col_block]
        for m in range(groups):
            out_ref[m, j] = part


def fold_call(tall, down, partner, shape):
    vmem = pl.BlockSpec(memory_space=pltpu.VMEM)
    close = functools.partial(pltpu.with_memory_space_constraint, memory_space=pltpu.VMEM)
    return pl.pallas_call(
        fold_kernel,
        out_shape=pltpu.VMEM(shape, tall.dtype),
        in_specs=[vmem] * 3,
        out_specs=vmem,
        compiler_params=pltpu.CompilerParams(vmem_limit_bytes=8 * 2**20),
    )(close(tall), close(down), close(partner))


def unfold_rows(x, width):
    pieces = [x[: min(FOLD, width - start)] for start in range(0, width, FOLD)]
    return jnp.concatenate(pieces, axis=0)


def ladder_kernel(
    cols,
    group,
    lane_group,
    pair_ref,
    t_ref,
    near_ref,
    far_ref,
    down_ref,
    across_ref,
    out_ref,
    inner,
    amp,
    ladders,
    side,
    stack,
    arrived,
):
    width = down_ref.shape[0]
    half_depth = near_ref.shape[0]
    groups, pairs_here = t_ref.shape[0] // cols, t_ref.shape[1]
    pairs = groups * pairs_here
    tiles = -(-width // FOLD)
    block = width // cols
    step = group * width
    half_steps = half_depth // step

    fetch = pltpu.make_async_copy(far_ref, stack, arrived)
    fetch.start()
    filler = jnp.full((1, tiles * FOLD - width), -1, jnp.int32)
    mixed = jnp.bitwise_xor(
        down_ref[...], jnp.concatenate([across_ref[...], filler], axis=1)
    )
    for p in range(pairs):
        half, at = p // pairs_here, p % pairs_here
        rows = jnp.concatenate(
            [t_ref[q * groups + half, at].astype(jnp.float32) for q in range(cols)], axis=0
        )
        spread = jnp.where(mixed == pair_ref[p : p + 1, :1], jnp.concatenate([rows] * tiles, axis=1), 0.0)
        amp[p * width : (p + 1) * width, :] = spread.astype(jnp.bfloat16)[:, :width]

    for source, base in ((near_ref, 0), (stack, half_steps)):
        if base:
            fetch.wait()

        @pl.loop(0, half_steps)
        def _(g, source=source, base=base):
            here = pl.multiple_of(g * step, step)
            there = pl.multiple_of((base + g) * step, step)
            for k in range(group):
                side[base + g, :, k * width : (k + 1) * width] = source[
                    pl.ds(pl.multiple_of(here + k * width, width), width), :
                ]
            part = lax.dot_general(
                amp[...],
                source[pl.ds(here, step), :],
                (((1,), (1,)), ((), ())),
                preferred_element_type=jnp.float32,
            ).astype(jnp.bfloat16)
            for p in range(pairs):
                for k in range(group):
                    inner[
                        pl.ds(pl.multiple_of(there + k * width, width), width),
                        p * width : (p + 1) * width,
                    ] = part[p * width : (p + 1) * width, k * width : (k + 1) * width]

    for start in range(0, pairs * width, lane_group):
        lanes = slice(start, start + lane_group)
        total = None
        for g in range(2 * half_steps):
            term = jnp.dot(
                side[g], inner[g * step : (g + 1) * step, lanes], preferred_element_type=jnp.float32
            )
            total = term if total is None else total + term
        ladders[:, lanes] = total

    for p in range(pairs):
        half, at = p // pairs_here, p % pairs_here
        ladder = ladders[:, p * width : (p + 1) * width]
        both = ladder + ladder.T
        both = jnp.concatenate(
            [both, jnp.zeros((width, tiles * FOLD - width), jnp.float32)], axis=1
        )
        both = jnp.where(mixed == pair_ref[p : p + 1, :1], both, 0.0)
        folded = both[:, :FOLD]
        for k in range(1, tiles):
            folded = folded + both[:, k * FOLD : (k + 1) * FOLD]
        for q in range(cols):
            out_ref[q * groups + half, at] = folded[q * block : (q + 1) * block].astype(
                out_ref.dtype
            )


def ladder_call(gathered, near, far, down, across, pair_labels, cols):
    count, width, _ = near.shape
    pairs = pair_labels.shape[0]
    group = 4
    depth, lanes = 2 * count * width, pairs * width
    vmem = pl.BlockSpec(memory_space=pltpu.VMEM)
    anywhere = pl.BlockSpec(memory_space=pl.ANY)
    close = functools.partial(pltpu.with_memory_space_constraint, memory_space=pltpu.VMEM)
    return pl.pallas_call(
        functools.partial(ladder_kernel, cols, group, 2 * FOLD),
        out_shape=pltpu.VMEM(gathered.shape, jnp.bfloat16),
        in_specs=[vmem, vmem, vmem, anywhere, vmem, vmem],
        out_specs=vmem,
        scratch_shapes=[
            pltpu.VMEM((depth, lanes), jnp.bfloat16),
            pltpu.VMEM((lanes, width), jnp.bfloat16),
            pltpu.VMEM((width, lanes), jnp.float32),
            pltpu.VMEM((2 * count // group, width, group * width), jnp.bfloat16),
            pltpu.VMEM((count * width, width), jnp.bfloat16),
            pltpu.SemaphoreType.DMA(()),
        ],
        compiler_params=pltpu.CompilerParams(vmem_limit_bytes=40 * 2**20),
    )(
        close(jnp.broadcast_to(pair_labels[:, None], (pairs, FOLD))),
        close(gathered),
        close(near.reshape(count * width, width)),
        pltpu.with_memory_space_constraint(far.reshape(count * width, width), pltpu.HBM),
        close(down),
        close(across),
    )


def body(amplitudes, factors, vir_irrep, pair_irrep):
    row_block, pairs_here, col_block = amplitudes.shape
    width = vir_irrep.shape[0]
    rows, cols = width // row_block, width // col_block
    held = pairs_here // CORES
    inner = held * col_block
    plane = ("col", "pair")
    core = lax.axis_index("row") % CORES
    swap = [(k, k ^ 1) for k in range(rows)]

    other_factors = lax.ppermute(factors, "row", swap)

    col_labels = lax.dynamic_slice_in_dim(vir_irrep, lax.axis_index("col") * col_block, col_block)
    pairs_held = lax.dynamic_slice_in_dim(pair_irrep, core * held, held)
    partner = jnp.bitwise_xor(pairs_held[:, None], col_labels[None, :]).reshape(1, inner)
    down = vir_irrep[:, None]

    halves = amplitudes.reshape(row_block, CORES, inner).transpose(1, 0, 2)
    sent = jnp.broadcast_to(halves[None], (rows // CORES, CORES, row_block, inner))
    sent = sent.reshape(rows, row_block, inner)
    tall = lax.all_to_all(sent, "row", 0, 0, tiled=True)
    groups = cols * lax.axis_size("pair")
    block = fold_call(tall, down, partner, (groups, held, col_block, FOLD))
    block, late_vir, late_pair = lax.optimization_barrier((block, vir_irrep, pair_irrep))
    gathered = lax.all_to_all(block, plane, 0, 0, tiled=True)

    other_pairs = lax.ppermute(late_pair, "pair", [(0, 1), (1, 0)])
    first = lax.axis_index("pair") == 0
    pair_labels = jnp.stack(
        [jnp.where(first, late_pair, other_pairs), jnp.where(first, other_pairs, late_pair)]
    )
    pair_labels = lax.dynamic_slice_in_dim(pair_labels, core * held, held, axis=1).reshape(-1)
    across = late_vir[None, :]
    row_labels = lax.dynamic_slice_in_dim(late_vir, lax.axis_index("row") * row_block, row_block)

    partial_sums = ladder_call(gathered, other_factors, factors, down, across, pair_labels, cols)

    pieces = lax.all_to_all(partial_sums, plane, 0, 0, tiled=True)
    summed = jnp.sum(pieces.astype(jnp.float32), axis=0).reshape(inner, FOLD)
    tall_sum = unfold_rows(summed.T, width).reshape(rows, row_block, inner)
    mixed = jnp.bitwise_xor(row_labels[:, None, None], col_labels[None, None, :])
    allowed = mixed == pair_irrep[None, :, None]
    tall_sum, allowed = lax.optimization_barrier((tall_sum, allowed))
    finals = lax.all_to_all(tall_sum, "row", 0, 0, tiled=True)
    ladder = jnp.sum(finals.reshape(rows // CORES, CORES, row_block, inner), axis=0)
    ladder = ladder.transpose(1, 0, 2).reshape(row_block, pairs_here, col_block)
    return jnp.where(allowed, ladder, jnp.zeros_like(ladder))


def solution(mesh):
    placed = (P("row", "pair", "col"), P(("row", "col", "pair"), None, None), P(), P("pair"))
    return jax.shard_map(
        body, mesh=mesh, in_specs=placed, out_specs=P("row", "pair", "col"), check_vma=False
    )
```

```python
import functools

import jax
import jax.numpy as jnp
from jax import lax
from jax.experimental import pallas as pl
from jax.experimental.pallas import tpu as pltpu
from jax.sharding import PartitionSpec as P


FOLD = 128
CORES = 2


def fold_kernel(tall_ref, down_ref, partner_ref, out_ref):
    groups, held, col_block, _ = out_ref.shape
    tall = jnp.concatenate(
        [tall_ref[r].astype(jnp.float32) for r in range(tall_ref.shape[0])], axis=0
    )
    tall = jnp.where(down_ref[...] == partner_ref[...], tall, 0.0)
    folded = tall[:FOLD]
    for start in range(FOLD, tall.shape[0], FOLD):
        piece = tall[start : start + FOLD]
        short = FOLD - piece.shape[0]
        if short:
            piece = jnp.concatenate([piece, jnp.zeros((short, piece.shape[1]), jnp.float32)], axis=0)
        folded = folded + piece
    block = folded.T.astype(out_ref.dtype)
    for j in range(held):
        part = block[j * col_block : (j + 1) * col_block]
        for m in range(groups):
            out_ref[m, j] = part


def fold_call(tall, down, partner, shape):
    vmem = pl.BlockSpec(memory_space=pltpu.VMEM)
    close = functools.partial(pltpu.with_memory_space_constraint, memory_space=pltpu.VMEM)
    return pl.pallas_call(
        fold_kernel,
        out_shape=pltpu.VMEM(shape, tall.dtype),
        in_specs=[vmem] * 3,
        out_specs=vmem,
        compiler_params=pltpu.CompilerParams(vmem_limit_bytes=8 * 2**20),
    )(close(tall), close(down), close(partner))


PACK = 16


def pack_kernel(row_block, pieces_ref, out_ref):
    total = pieces_ref[0].astype(jnp.float32)
    for m in range(1, pieces_ref.shape[0]):
        total = total + pieces_ref[m].astype(jnp.float32)
    total = total.reshape(-1, FOLD)
    lane = lax.broadcasted_iota(jnp.int32, (PACK, FOLD), 1)
    for r in range(out_ref.shape[0]):
        packed = jnp.zeros((PACK, FOLD), jnp.float32)
        for g in range(total.shape[0] // PACK):
            shift = (g - r) * row_block % FOLD
            moved = total[g * PACK : (g + 1) * PACK]
            if shift:
                moved = pltpu.roll(moved, shift, 1)
            packed = jnp.where(
                (lane >= g * row_block) & (lane < (g + 1) * row_block), moved, packed
            )
        out_ref[r] = packed


def unpack_kernel(finals_ref, down_ref, across_ref, out_ref):
    row_block, pairs_here, col_block = out_ref.shape
    held = pairs_here // CORES
    lines = held * col_block
    for c in range(CORES):
        total = finals_ref[c]
        for z in range(CORES + c, finals_ref.shape[0], CORES):
            total = total + finals_ref[z]
        spread = jnp.concatenate(
            [
                total if g == 0 else pltpu.roll(total, -g * row_block % FOLD, 1)
                for g in range(lines // PACK)
            ],
            axis=0,
        )
        spread = jnp.where(
            down_ref[:, :1] == across_ref[c : c + 1, :lines], spread.T[:row_block], 0.0
        )
        for j in range(held):
            out_ref[:, c * held + j, :] = spread[:, j * col_block : (j + 1) * col_block]


def pack_call(pieces, rows, row_block):
    close = functools.partial(pltpu.with_memory_space_constraint, memory_space=pltpu.VMEM)
    vmem = pl.BlockSpec(memory_space=pltpu.VMEM)
    return pl.pallas_call(
        functools.partial(pack_kernel, row_block),
        out_shape=jax.ShapeDtypeStruct((rows, PACK, FOLD), jnp.float32),
        in_specs=[vmem],
        out_specs=vmem,
        compiler_params=pltpu.CompilerParams(vmem_limit_bytes=8 * 2**20),
    )(close(pieces))


def unpack_call(finals, down, across, shape):
    close = functools.partial(pltpu.with_memory_space_constraint, memory_space=pltpu.VMEM)
    vmem = pl.BlockSpec(memory_space=pltpu.VMEM)
    return pl.pallas_call(
        unpack_kernel,
        out_shape=jax.ShapeDtypeStruct(shape, jnp.float32),
        in_specs=[vmem] * 3,
        out_specs=vmem,
        compiler_params=pltpu.CompilerParams(vmem_limit_bytes=8 * 2**20),
    )(close(finals), close(down), close(across))


def ladder_kernel(
    cols,
    group,
    lane_group,
    pair_ref,
    t_ref,
    near_ref,
    far_ref,
    down_ref,
    across_ref,
    out_ref,
    inner,
    amp,
    ladders,
    side,
    stack,
    arrived,
):
    width = down_ref.shape[0]
    half_depth = near_ref.shape[0]
    groups, pairs_here = t_ref.shape[0] // cols, t_ref.shape[1]
    pairs = groups * pairs_here
    tiles = -(-width // FOLD)
    block = width // cols
    step = group * width
    half_steps = half_depth // step

    fetch = pltpu.make_async_copy(far_ref, stack, arrived)
    fetch.start()
    filler = jnp.full((1, tiles * FOLD - width), -1, jnp.int32)
    mixed = jnp.bitwise_xor(
        down_ref[...], jnp.concatenate([across_ref[...], filler], axis=1)
    )
    for p in range(pairs):
        half, at = p // pairs_here, p % pairs_here
        rows = jnp.concatenate(
            [t_ref[q * groups + half, at].astype(jnp.float32) for q in range(cols)], axis=0
        )
        spread = jnp.where(mixed == pair_ref[p : p + 1, :1], jnp.concatenate([rows] * tiles, axis=1), 0.0)
        amp[p * width : (p + 1) * width, :] = spread.astype(jnp.bfloat16)[:, :width]

    for source, base in ((near_ref, 0), (stack, half_steps)):
        if base:
            fetch.wait()

        @pl.loop(0, half_steps)
        def _(g, source=source, base=base):
            here = pl.multiple_of(g * step, step)
            there = pl.multiple_of((base + g) * step, step)
            for k in range(group):
                side[base + g, :, k * width : (k + 1) * width] = source[
                    pl.ds(pl.multiple_of(here + k * width, width), width), :
                ]
            part = lax.dot_general(
                amp[...],
                source[pl.ds(here, step), :],
                (((1,), (1,)), ((), ())),
                preferred_element_type=jnp.float32,
            ).astype(jnp.bfloat16)
            for p in range(pairs):
                for k in range(group):
                    inner[
                        pl.ds(pl.multiple_of(there + k * width, width), width),
                        p * width : (p + 1) * width,
                    ] = part[p * width : (p + 1) * width, k * width : (k + 1) * width]

    for start in range(0, pairs * width, lane_group):
        lanes = slice(start, start + lane_group)
        total = None
        for g in range(2 * half_steps):
            term = jnp.dot(
                side[g], inner[g * step : (g + 1) * step, lanes], preferred_element_type=jnp.float32
            )
            total = term if total is None else total + term
        ladders[:, lanes] = total

    for p in range(pairs):
        half, at = p // pairs_here, p % pairs_here
        ladder = jnp.concatenate(
            [
                ladders[:, p * width : (p + 1) * width],
                jnp.zeros((width, tiles * FOLD - width), jnp.float32),
            ],
            axis=1,
        )
        ladder = jnp.where(mixed == pair_ref[p : p + 1, :1], ladder, 0.0)
        folded = ladder[:, :FOLD]
        tall = ladder[:FOLD]
        for start in range(FOLD, tiles * FOLD, FOLD):
            folded = folded + ladder[:, start : start + FOLD]
            piece = ladder[start : start + FOLD]
            if piece.shape[0] < FOLD:
                blank = jnp.zeros((FOLD - piece.shape[0], tiles * FOLD), jnp.float32)
                piece = jnp.concatenate([piece, blank], axis=0)
            tall = tall + piece
        folded = folded + tall.T[:width]
        for q in range(cols):
            out_ref[q * groups + half, at] = folded[q * block : (q + 1) * block].astype(
                out_ref.dtype
            )


def ladder_call(gathered, near, far, down, across, pair_labels, cols):
    count, width, _ = near.shape
    pairs = pair_labels.shape[0]
    group = 4
    depth, lanes = 2 * count * width, pairs * width
    vmem = pl.BlockSpec(memory_space=pltpu.VMEM)
    anywhere = pl.BlockSpec(memory_space=pl.ANY)
    close = functools.partial(pltpu.with_memory_space_constraint, memory_space=pltpu.VMEM)
    return pl.pallas_call(
        functools.partial(ladder_kernel, cols, group, 2 * FOLD),
        out_shape=pltpu.VMEM(gathered.shape, jnp.bfloat16),
        in_specs=[vmem, vmem, vmem, anywhere, vmem, vmem],
        out_specs=vmem,
        scratch_shapes=[
            pltpu.VMEM((depth, lanes), jnp.bfloat16),
            pltpu.VMEM((lanes, width), jnp.bfloat16),
            pltpu.VMEM((width, lanes), jnp.float32),
            pltpu.VMEM((2 * count // group, width, group * width), jnp.bfloat16),
            pltpu.VMEM((count * width, width), jnp.bfloat16),
            pltpu.SemaphoreType.DMA(()),
        ],
        compiler_params=pltpu.CompilerParams(vmem_limit_bytes=40 * 2**20),
    )(
        close(jnp.broadcast_to(pair_labels[:, None], (pairs, FOLD))),
        close(gathered),
        close(near.reshape(count * width, width)),
        pltpu.with_memory_space_constraint(far.reshape(count * width, width), pltpu.HBM),
        close(down),
        close(across),
    )


def body(amplitudes, factors, vir_irrep, pair_irrep):
    row_block, pairs_here, col_block = amplitudes.shape
    width = vir_irrep.shape[0]
    rows, cols = width // row_block, width // col_block
    held = pairs_here // CORES
    inner = held * col_block
    plane = ("col", "pair")
    core = lax.axis_index("row") % CORES
    swap = [(k, k ^ 1) for k in range(rows)]

    other_factors = lax.ppermute(factors, "row", swap)

    col_labels = lax.dynamic_slice_in_dim(vir_irrep, lax.axis_index("col") * col_block, col_block)
    pairs_held = lax.dynamic_slice_in_dim(pair_irrep, core * held, held)
    partner = jnp.bitwise_xor(pairs_held[:, None], col_labels[None, :]).reshape(1, inner)
    down = vir_irrep[:, None]

    halves = amplitudes.reshape(row_block, CORES, inner).transpose(1, 0, 2)
    sent = jnp.broadcast_to(halves[None], (rows // CORES, CORES, row_block, inner))
    sent = sent.reshape(rows, row_block, inner)
    tall = lax.all_to_all(sent, "row", 0, 0, tiled=True)
    groups = cols * lax.axis_size("pair")
    block = fold_call(tall, down, partner, (groups, held, col_block, FOLD))
    block, late_vir, late_pair = lax.optimization_barrier((block, vir_irrep, pair_irrep))
    gathered = lax.all_to_all(block, plane, 0, 0, tiled=True)

    other_pairs = lax.ppermute(late_pair, "pair", [(0, 1), (1, 0)])
    first = lax.axis_index("pair") == 0
    pair_labels = jnp.stack(
        [jnp.where(first, late_pair, other_pairs), jnp.where(first, other_pairs, late_pair)]
    )
    pair_labels = lax.dynamic_slice_in_dim(pair_labels, core * held, held, axis=1).reshape(-1)
    across = late_vir[None, :]
    row_labels = lax.dynamic_slice_in_dim(late_vir, lax.axis_index("row") * row_block, row_block)

    partial_sums = ladder_call(gathered, other_factors, factors, down, across, pair_labels, cols)

    pieces = lax.all_to_all(partial_sums, plane, 0, 0, tiled=True)
    packed = pack_call(pieces, rows, row_block)
    need = jnp.bitwise_xor(pair_irrep[:, None], col_labels[None, :]).reshape(CORES, inner)
    packed, row_labels, need = lax.optimization_barrier(
        (packed, jnp.broadcast_to(row_labels[:, None], (row_block, FOLD)), need)
    )
    finals = lax.all_to_all(packed, "row", 0, 0, tiled=True)
    return unpack_call(finals, row_labels, need, amplitudes.shape)


def solution(mesh):
    placed = (P("row", "pair", "col"), P(("row", "col", "pair"), None, None), P(), P("pair"))
    return jax.shard_map(
        body, mesh=mesh, in_specs=placed, out_specs=P("row", "pair", "col"), check_vma=False
    )
```

```python
import functools

import jax
import jax.numpy as jnp
from jax import lax
from jax.experimental import pallas as pl
from jax.experimental.pallas import tpu as pltpu
from jax.sharding import PartitionSpec as P


FOLD = 128
CORES = 2


PACK = 16


def spread_kernel(amp_ref, out_ref):
    row_block, pairs_here, col_block = amp_ref.shape
    held = pairs_here // CORES
    lines = held * col_block
    amp = amp_ref[...].astype(jnp.float32)
    for c in range(CORES):
        lane_side = jnp.concatenate([amp[:, c * held + j, :] for j in range(held)], axis=1)
        column = lane_side.T
        groups = [column[g * PACK : (g + 1) * PACK] for g in range(lines // PACK)]
        rest = FOLD - row_block * len(groups)
        groups.append(jnp.zeros((PACK, rest), jnp.float32))
        packed = jnp.concatenate(groups, axis=1).astype(out_ref.dtype)
        for m in range(c, out_ref.shape[0], CORES):
            out_ref[m] = packed


def fold_kernel(row_block, tall_ref, across_ref, partner_ref, out_ref):
    groups, held, col_block, _ = out_ref.shape
    width = across_ref.shape[1]
    lines = held * col_block
    tiles = -(-width // FOLD)
    filler = jnp.full((1, tiles * FOLD - width), -1, jnp.int32)
    labels = jnp.concatenate([across_ref[...], filler], axis=1)
    partner = jnp.broadcast_to(partner_ref[...], (8, lines)).T[:, :1]
    lane = lax.broadcasted_iota(jnp.int32, (1, FOLD), 1)
    folded = [jnp.zeros((PACK, FOLD), jnp.float32) for _ in range(lines // PACK)]
    for r in range(tall_ref.shape[0]):
        tile, low = r * row_block // FOLD, r * row_block % FOLD
        here = jnp.where(
            (lane >= low) & (lane < low + row_block), labels[:, tile * FOLD : (tile + 1) * FOLD], -1
        )
        over = low + row_block - FOLD
        if over > 0:
            following = labels[:, (tile + 1) * FOLD : (tile + 2) * FOLD]
            here = jnp.where(lane < over, following, here)
        piece = tall_ref[r].astype(jnp.float32)
        for g in range(lines // PACK):
            shift = (r - g) * row_block % FOLD
            moved = pltpu.roll(piece, shift, 1) if shift else piece
            fits = partner[g * PACK : (g + 1) * PACK] == here
            folded[g] = folded[g] + jnp.where(fits, moved, 0.0)
    block = jnp.concatenate(folded, axis=0)
    for j in range(held):
        part = block[j * col_block : (j + 1) * col_block].astype(out_ref.dtype)
        for m in range(groups):
            out_ref[m, j] = part


def spread_call(amplitudes, rows):
    vmem = pl.BlockSpec(memory_space=pltpu.VMEM)
    return pl.pallas_call(
        spread_kernel,
        out_shape=jax.ShapeDtypeStruct((rows, PACK, FOLD), amplitudes.dtype),
        in_specs=[vmem],
        out_specs=vmem,
        compiler_params=pltpu.CompilerParams(vmem_limit_bytes=8 * 2**20),
    )(amplitudes)


def fold_call(tall, across, partner, row_block, shape):
    vmem = pl.BlockSpec(memory_space=pltpu.VMEM)
    close = functools.partial(pltpu.with_memory_space_constraint, memory_space=pltpu.VMEM)
    return pl.pallas_call(
        functools.partial(fold_kernel, row_block),
        out_shape=jax.ShapeDtypeStruct(shape, tall.dtype),
        in_specs=[vmem] * 3,
        out_specs=vmem,
        compiler_params=pltpu.CompilerParams(vmem_limit_bytes=8 * 2**20),
    )(close(tall), close(across), close(partner))


def pack_kernel(row_block, pieces_ref, out_ref):
    total = pieces_ref[0].astype(jnp.float32)
    for m in range(1, pieces_ref.shape[0]):
        total = total + pieces_ref[m].astype(jnp.float32)
    total = total.reshape(-1, FOLD)
    lane = lax.broadcasted_iota(jnp.int32, (PACK, FOLD), 1)
    for r in range(out_ref.shape[0]):
        packed = jnp.zeros((PACK, FOLD), jnp.float32)
        for g in range(total.shape[0] // PACK):
            shift = (g - r) * row_block % FOLD
            moved = total[g * PACK : (g + 1) * PACK]
            if shift:
                moved = pltpu.roll(moved, shift, 1)
            packed = jnp.where(
                (lane >= g * row_block) & (lane < (g + 1) * row_block), moved, packed
            )
        out_ref[r] = packed


def unpack_kernel(finals_ref, down_ref, across_ref, out_ref):
    row_block, pairs_here, col_block = out_ref.shape
    held = pairs_here // CORES
    lines = held * col_block
    for c in range(CORES):
        total = finals_ref[c]
        for z in range(CORES + c, finals_ref.shape[0], CORES):
            total = total + finals_ref[z]
        spread = jnp.concatenate(
            [
                total if g == 0 else pltpu.roll(total, -g * row_block % FOLD, 1)
                for g in range(lines // PACK)
            ],
            axis=0,
        )
        spread = jnp.where(
            down_ref[:, :1] == across_ref[c : c + 1, :lines], spread.T[:row_block], 0.0
        )
        for j in range(held):
            out_ref[:, c * held + j, :] = spread[:, j * col_block : (j + 1) * col_block]


def pack_call(pieces, rows, row_block):
    close = functools.partial(pltpu.with_memory_space_constraint, memory_space=pltpu.VMEM)
    vmem = pl.BlockSpec(memory_space=pltpu.VMEM)
    return pl.pallas_call(
        functools.partial(pack_kernel, row_block),
        out_shape=jax.ShapeDtypeStruct((rows, PACK, FOLD), jnp.float32),
        in_specs=[vmem],
        out_specs=vmem,
        compiler_params=pltpu.CompilerParams(vmem_limit_bytes=8 * 2**20),
    )(close(pieces))


def unpack_call(finals, down, across, shape):
    close = functools.partial(pltpu.with_memory_space_constraint, memory_space=pltpu.VMEM)
    vmem = pl.BlockSpec(memory_space=pltpu.VMEM)
    return pl.pallas_call(
        unpack_kernel,
        out_shape=jax.ShapeDtypeStruct(shape, jnp.float32),
        in_specs=[vmem] * 3,
        out_specs=vmem,
        compiler_params=pltpu.CompilerParams(vmem_limit_bytes=8 * 2**20),
    )(close(finals), close(down), close(across))


def ladder_kernel(
    cols,
    group,
    lane_group,
    pair_ref,
    t_ref,
    near_ref,
    far_ref,
    across_ref,
    out_ref,
    inner,
    amp,
    ladders,
    side,
    stack,
    arrived,
):
    width = across_ref.shape[1]
    half_depth = near_ref.shape[0]
    groups, pairs_here = t_ref.shape[0] // cols, t_ref.shape[1]
    pairs = groups * pairs_here
    tiles = -(-width // FOLD)
    block = width // cols
    step = group * width
    half_steps = half_depth // step

    fetch = pltpu.make_async_copy(far_ref, stack, arrived)
    fetch.start()
    filler = jnp.full((1, tiles * FOLD - width), -1, jnp.int32)
    down = jnp.broadcast_to(across_ref[...], (8, width)).T[:, :1]
    mixed = jnp.bitwise_xor(down, jnp.concatenate([across_ref[...], filler], axis=1))
    for p in range(pairs):
        half, at = p // pairs_here, p % pairs_here
        rows = jnp.concatenate(
            [t_ref[q * groups + half, at].astype(jnp.float32) for q in range(cols)], axis=0
        )
        spread = jnp.where(mixed == pair_ref[p : p + 1, :1], jnp.concatenate([rows] * tiles, axis=1), 0.0)
        amp[p * width : (p + 1) * width, :] = spread.astype(jnp.bfloat16)[:, :width]

    for source, base in ((near_ref, 0), (stack, half_steps)):
        if base:
            fetch.wait()

        @pl.loop(0, half_steps)
        def _(g, source=source, base=base):
            here = pl.multiple_of(g * step, step)
            there = pl.multiple_of((base + g) * step, step)
            for k in range(group):
                side[base + g, :, k * width : (k + 1) * width] = source[
                    pl.ds(pl.multiple_of(here + k * width, width), width), :
                ]
            part = lax.dot_general(
                amp[...],
                source[pl.ds(here, step), :],
                (((1,), (1,)), ((), ())),
                preferred_element_type=jnp.float32,
            ).astype(jnp.bfloat16)
            for p in range(pairs):
                for k in range(group):
                    inner[
                        pl.ds(pl.multiple_of(there + k * width, width), width),
                        p * width : (p + 1) * width,
                    ] = part[p * width : (p + 1) * width, k * width : (k + 1) * width]

    for start in range(0, pairs * width, lane_group):
        lanes = slice(start, start + lane_group)
        total = None
        for g in range(2 * half_steps):
            term = jnp.dot(
                side[g], inner[g * step : (g + 1) * step, lanes], preferred_element_type=jnp.float32
            )
            total = term if total is None else total + term
        ladders[:, lanes] = total

    for p in range(pairs):
        half, at = p // pairs_here, p % pairs_here
        ladder = jnp.concatenate(
            [
                ladders[:, p * width : (p + 1) * width],
                jnp.zeros((width, tiles * FOLD - width), jnp.float32),
            ],
            axis=1,
        )
        ladder = jnp.where(mixed == pair_ref[p : p + 1, :1], ladder, 0.0)
        folded = ladder[:, :FOLD]
        tall = ladder[:FOLD]
        for start in range(FOLD, tiles * FOLD, FOLD):
            folded = folded + ladder[:, start : start + FOLD]
            piece = ladder[start : start + FOLD]
            if piece.shape[0] < FOLD:
                blank = jnp.zeros((FOLD - piece.shape[0], tiles * FOLD), jnp.float32)
                piece = jnp.concatenate([piece, blank], axis=0)
            tall = tall + piece
        folded = folded + tall.T[:width]
        for q in range(cols):
            out_ref[q * groups + half, at] = folded[q * block : (q + 1) * block].astype(
                out_ref.dtype
            )


def ladder_call(gathered, near, far, across, pair_labels, cols):
    count, width, _ = near.shape
    pairs = pair_labels.shape[0]
    group = 4
    depth, lanes = 2 * count * width, pairs * width
    vmem = pl.BlockSpec(memory_space=pltpu.VMEM)
    anywhere = pl.BlockSpec(memory_space=pl.ANY)
    close = functools.partial(pltpu.with_memory_space_constraint, memory_space=pltpu.VMEM)
    return pl.pallas_call(
        functools.partial(ladder_kernel, cols, group, 2 * FOLD),
        out_shape=pltpu.VMEM(gathered.shape, jnp.bfloat16),
        in_specs=[vmem, vmem, vmem, anywhere, vmem],
        out_specs=vmem,
        scratch_shapes=[
            pltpu.VMEM((depth, lanes), jnp.bfloat16),
            pltpu.VMEM((lanes, width), jnp.bfloat16),
            pltpu.VMEM((width, lanes), jnp.float32),
            pltpu.VMEM((2 * count // group, width, group * width), jnp.bfloat16),
            pltpu.VMEM((count * width, width), jnp.bfloat16),
            pltpu.SemaphoreType.DMA(()),
        ],
        compiler_params=pltpu.CompilerParams(vmem_limit_bytes=40 * 2**20),
    )(
        close(jnp.broadcast_to(pair_labels[:, None], (pairs, FOLD))),
        close(gathered),
        close(near.reshape(count * width, width)),
        pltpu.with_memory_space_constraint(far.reshape(count * width, width), pltpu.HBM),
        close(across),
    )


def body(amplitudes, factors, vir_irrep, pair_irrep):
    row_block, pairs_here, col_block = amplitudes.shape
    width = vir_irrep.shape[0]
    rows, cols = width // row_block, width // col_block
    held = pairs_here // CORES
    inner = held * col_block
    plane = ("col", "pair")
    core = lax.axis_index("row") % CORES
    swap = [(k, k ^ 1) for k in range(rows)]

    other_factors = lax.ppermute(factors, "row", swap)

    col_labels = lax.dynamic_slice_in_dim(vir_irrep, lax.axis_index("col") * col_block, col_block)
    pairs_held = lax.dynamic_slice_in_dim(pair_irrep, core * held, held)
    partner = jnp.bitwise_xor(pairs_held[:, None], col_labels[None, :]).reshape(1, inner)
    across = vir_irrep[None, :]

    sent = spread_call(amplitudes, rows)
    tall = lax.all_to_all(sent, "row", 0, 0, tiled=True)
    groups = cols * lax.axis_size("pair")
    block = fold_call(tall, across, partner, row_block, (groups, held, col_block, FOLD))
    block, late_vir, late_pair = lax.optimization_barrier((block, vir_irrep, pair_irrep))
    gathered = lax.all_to_all(block, plane, 0, 0, tiled=True)

    other_pairs = lax.ppermute(late_pair, "pair", [(0, 1), (1, 0)])
    first = lax.axis_index("pair") == 0
    pair_labels = jnp.stack(
        [jnp.where(first, late_pair, other_pairs), jnp.where(first, other_pairs, late_pair)]
    )
    pair_labels = lax.dynamic_slice_in_dim(pair_labels, core * held, held, axis=1).reshape(-1)
    row_labels = lax.dynamic_slice_in_dim(late_vir, lax.axis_index("row") * row_block, row_block)

    partial_sums = ladder_call(gathered, other_factors, factors, across, pair_labels, cols)

    pieces = lax.all_to_all(partial_sums, plane, 0, 0, tiled=True)
    packed = pack_call(pieces, rows, row_block)
    need = jnp.bitwise_xor(pair_irrep[:, None], col_labels[None, :]).reshape(CORES, inner)
    packed, row_labels, need = lax.optimization_barrier(
        (packed, jnp.broadcast_to(row_labels[:, None], (row_block, FOLD)), need)
    )
    finals = lax.all_to_all(packed, "row", 0, 0, tiled=True)
    return unpack_call(finals, row_labels, need, amplitudes.shape)


def solution(mesh):
    placed = (P("row", "pair", "col"), P(("row", "col", "pair"), None, None), P(), P("pair"))
    return jax.shard_map(
        body, mesh=mesh, in_specs=placed, out_specs=P("row", "pair", "col"), check_vma=False
    )
```

```python
import functools

import jax
import jax.numpy as jnp
from jax import lax
from jax.experimental import pallas as pl
from jax.experimental.pallas import tpu as pltpu
from jax.sharding import PartitionSpec as P


LANES = 128
FOLD = 80
LEFT = LANES - FOLD
REST = FOLD - LEFT
SUB = 8
CORES = 2


def lanes():
    return lax.broadcasted_iota(jnp.int32, (1, LANES), 1)


def turn(x, shift):
    shift = shift % LANES
    return pltpu.roll(x, shift, 1) if shift else x


def join(first, second):
    lane = lanes()
    block = second.shape[0]
    main = jnp.where(lane < FOLD, first, turn(second, FOLD))
    rows, per_row = [], LANES // REST
    for start in range(0, block // SUB, per_row):
        row = jnp.zeros((SUB, LANES), jnp.float32)
        for k in range(min(per_row, block // SUB - start)):
            at = (start + k) * SUB
            moved = turn(second[at : at + SUB], k * REST - LEFT)
            row = jnp.where((lane >= k * REST) & (lane < (k + 1) * REST), moved, row)
        rows.append(row)
    return jnp.concatenate([main] + rows, axis=0)


def joined_rows(block):
    return block + -(-(block // SUB) // (LANES // REST)) * SUB


def part(x, block):
    lane = lanes()
    per_row = LANES // REST
    first = x[:block]
    tail = [
        turn(
            x[block + g // per_row * SUB : block + (g // per_row + 1) * SUB],
            LEFT - g % per_row * REST,
        )
        for g in range(block // SUB)
    ]
    second = jnp.where(lane < LEFT, turn(first, -FOLD), jnp.concatenate(tail, axis=0))
    return first, second


def unfold(x, tiles):
    lane = lanes()
    out = []
    for t in range(tiles):
        base = t * LANES
        tile = None
        for m in range(base // FOLD, -(-(base + LANES) // FOLD)):
            moved = turn(x, m * FOLD - base)
            tile = moved if tile is None else jnp.where(lane >= m * FOLD - base, moved, tile)
        out.append(tile)
    return out


def fold(pieces):
    lane = lanes()
    total, by_shift = None, {}
    for t, piece in enumerate(pieces):
        base = t * LANES
        for m in range(base // FOLD, -(-(base + LANES) // FOLD)):
            low, high = max(m * FOLD - base, 0), min((m + 1) * FOLD - base, LANES)
            inside = jnp.where((lane >= low) & (lane < high), piece, 0.0)
            shift = (base - m * FOLD) % LANES
            by_shift[shift] = inside if shift not in by_shift else by_shift[shift] + inside
    for shift, piece in by_shift.items():
        moved = turn(piece, shift)
        total = moved if total is None else total + moved
    return total


PACK = 16


def spread_kernel(amp_ref, out_ref):
    row_block, pairs_here, col_block = amp_ref.shape
    held = pairs_here // CORES
    lines = held * col_block
    amp = amp_ref[...].astype(jnp.float32)
    for c in range(CORES):
        lane_side = jnp.concatenate([amp[:, c * held + j, :] for j in range(held)], axis=1)
        column = lane_side.T
        groups = [column[g * PACK : (g + 1) * PACK] for g in range(lines // PACK)]
        rest = LANES - row_block * len(groups)
        groups.append(jnp.zeros((PACK, rest), jnp.float32))
        packed = jnp.concatenate(groups, axis=1).astype(out_ref.dtype)
        for m in range(c, out_ref.shape[0], CORES):
            out_ref[m] = packed


def fold_kernel(row_block, col_block, tall_ref, across_ref, partner_ref, out_ref):
    width = across_ref.shape[1]
    lines = partner_ref.shape[1]
    partner = jnp.broadcast_to(partner_ref[...], (SUB, lines)).T[:, :1]
    lane = lanes()
    filler = jnp.full((1, LANES - FOLD), -1, jnp.int32)
    folded = [jnp.zeros((PACK, LANES), jnp.float32) for _ in range(lines // PACK)]
    for m in range(width // FOLD):
        labels = jnp.concatenate([across_ref[:, m * FOLD : (m + 1) * FOLD], filler], axis=1)
        for k in range(FOLD // row_block):
            low = k * row_block
            here = jnp.where((lane >= low) & (lane < low + row_block), labels, -1)
            piece = tall_ref[m * (FOLD // row_block) + k].astype(jnp.float32)
            for g in range(lines // PACK):
                fits = partner[g * PACK : (g + 1) * PACK] == here
                folded[g] = folded[g] + jnp.where(fits, turn(piece, (k - g) * row_block), 0.0)
    block = jnp.concatenate(folded, axis=0)
    block = join(block[:col_block], block[col_block:]).astype(out_ref.dtype)
    for m in range(out_ref.shape[0]):
        out_ref[m] = block


def spread_call(amplitudes, rows):
    vmem = pl.BlockSpec(memory_space=pltpu.VMEM)
    return pl.pallas_call(
        spread_kernel,
        out_shape=jax.ShapeDtypeStruct((rows, PACK, LANES), amplitudes.dtype),
        in_specs=[vmem],
        out_specs=vmem,
        compiler_params=pltpu.CompilerParams(vmem_limit_bytes=8 * 2**20),
    )(amplitudes)


def fold_call(tall, across, partner, row_block, col_block, groups):
    vmem = pl.BlockSpec(memory_space=pltpu.VMEM)
    close = functools.partial(pltpu.with_memory_space_constraint, memory_space=pltpu.VMEM)
    return pl.pallas_call(
        functools.partial(fold_kernel, row_block, col_block),
        out_shape=jax.ShapeDtypeStruct((groups, joined_rows(col_block), LANES), tall.dtype),
        in_specs=[vmem] * 3,
        out_specs=vmem,
        compiler_params=pltpu.CompilerParams(vmem_limit_bytes=8 * 2**20),
    )(close(tall), close(across), close(partner))


def pack_kernel(row_block, col_block, pieces_ref, out_ref):
    total = pieces_ref[0].astype(jnp.float32)
    for m in range(1, pieces_ref.shape[0]):
        total = total + pieces_ref[m].astype(jnp.float32)
    total = jnp.concatenate(part(total, col_block), axis=0)
    lane = lanes()
    period = FOLD // row_block
    for k in range(period):
        packed = jnp.zeros((PACK, LANES), jnp.float32)
        for g in range(total.shape[0] // PACK):
            moved = turn(total[g * PACK : (g + 1) * PACK], (g - k) * row_block)
            packed = jnp.where(
                (lane >= g * row_block) & (lane < (g + 1) * row_block), moved, packed
            )
        for r in range(k, out_ref.shape[0], period):
            out_ref[r] = packed


def unpack_kernel(finals_ref, down_ref, across_ref, out_ref):
    row_block, pairs_here, col_block = out_ref.shape
    held = pairs_here // CORES
    lines = held * col_block
    for c in range(CORES):
        total = finals_ref[c]
        for z in range(CORES + c, finals_ref.shape[0], CORES):
            total = total + finals_ref[z]
        spread = jnp.concatenate(
            [
                turn(total, -g * row_block)
                for g in range(lines // PACK)
            ],
            axis=0,
        )
        spread = jnp.where(
            down_ref[:, :1] == across_ref[c : c + 1, :lines], spread.T[:row_block], 0.0
        )
        for j in range(held):
            out_ref[:, c * held + j, :] = spread[:, j * col_block : (j + 1) * col_block]


def pack_call(pieces, rows, row_block, col_block):
    close = functools.partial(pltpu.with_memory_space_constraint, memory_space=pltpu.VMEM)
    vmem = pl.BlockSpec(memory_space=pltpu.VMEM)
    return pl.pallas_call(
        functools.partial(pack_kernel, row_block, col_block),
        out_shape=jax.ShapeDtypeStruct((rows, PACK, LANES), jnp.float32),
        in_specs=[vmem],
        out_specs=vmem,
        compiler_params=pltpu.CompilerParams(vmem_limit_bytes=8 * 2**20),
    )(close(pieces))


def unpack_call(finals, down, across, shape):
    close = functools.partial(pltpu.with_memory_space_constraint, memory_space=pltpu.VMEM)
    vmem = pl.BlockSpec(memory_space=pltpu.VMEM)
    return pl.pallas_call(
        unpack_kernel,
        out_shape=jax.ShapeDtypeStruct(shape, jnp.float32),
        in_specs=[vmem] * 3,
        out_specs=vmem,
        compiler_params=pltpu.CompilerParams(vmem_limit_bytes=8 * 2**20),
    )(close(finals), close(down), close(across))


def ladder_kernel(
    cols,
    group,
    lane_group,
    pair_ref,
    t_ref,
    near_ref,
    far_ref,
    across_ref,
    out_ref,
    inner,
    amp,
    ladders,
    side,
    stack,
    arrived,
):
    width = across_ref.shape[1]
    half_depth = near_ref.shape[0]
    groups, pairs = t_ref.shape[0] // cols, pair_ref.shape[0]
    tiles = -(-width // LANES)
    block = width // cols
    step = group * width
    half_steps = half_depth // step

    fetch = pltpu.make_async_copy(far_ref, stack, arrived)
    fetch.start()
    filler = jnp.full((1, tiles * LANES - width), -1, jnp.int32)
    down = jnp.broadcast_to(across_ref[...], (8, width)).T[:, :1]
    mixed = jnp.bitwise_xor(down, jnp.concatenate([across_ref[...], filler], axis=1))
    for half in range(groups):
        both = [part(t_ref[q * groups + half].astype(jnp.float32), block) for q in range(cols)]
        for at in range(CORES):
            p = half * CORES + at
            rows = jnp.concatenate([pieces[at] for pieces in both], axis=0)
            spread = jnp.concatenate(unfold(rows, tiles), axis=1)
            spread = jnp.where(mixed == pair_ref[p : p + 1, :1], spread, 0.0)
            amp[p * width : (p + 1) * width, :] = spread.astype(jnp.bfloat16)[:, :width]

    for source, base in ((near_ref, 0), (stack, half_steps)):
        if base:
            fetch.wait()

        @pl.loop(0, half_steps)
        def _(g, source=source, base=base):
            here = pl.multiple_of(g * step, step)
            there = pl.multiple_of((base + g) * step, step)
            for k in range(group):
                side[base + g, :, k * width : (k + 1) * width] = source[
                    pl.ds(pl.multiple_of(here + k * width, width), width), :
                ]
            part = lax.dot_general(
                amp[...],
                source[pl.ds(here, step), :],
                (((1,), (1,)), ((), ())),
                preferred_element_type=jnp.float32,
            ).astype(jnp.bfloat16)
            for p in range(pairs):
                for k in range(group):
                    inner[
                        pl.ds(pl.multiple_of(there + k * width, width), width),
                        p * width : (p + 1) * width,
                    ] = part[p * width : (p + 1) * width, k * width : (k + 1) * width]

    for start in range(0, pairs * width, lane_group):
        lanes = slice(start, start + lane_group)
        total = None
        for g in range(2 * half_steps):
            term = jnp.dot(
                side[g], inner[g * step : (g + 1) * step, lanes], preferred_element_type=jnp.float32
            )
            total = term if total is None else total + term
        ladders[:, lanes] = total

    blank = jnp.zeros((width, tiles * LANES - width), jnp.float32)
    for half in range(groups):
        both = []
        for at in range(CORES):
            p = half * CORES + at
            ladder = jnp.concatenate([ladders[:, p * width : (p + 1) * width], blank], axis=1)
            ladder = jnp.where(mixed == pair_ref[p : p + 1, :1], ladder, 0.0)
            tall = ladder[:FOLD]
            for start in range(FOLD, width, FOLD):
                tall = tall + ladder[start : start + FOLD]
            tall = jnp.concatenate(
                [tall, jnp.zeros((LANES - FOLD, tiles * LANES), jnp.float32)], axis=0
            )
            flat = fold([ladder[:, t * LANES : (t + 1) * LANES] for t in range(tiles)])
            both.append(flat + tall.T[:width])
        for q in range(cols):
            span = slice(q * block, (q + 1) * block)
            out_ref[q * groups + half] = join(both[0][span], both[1][span]).astype(out_ref.dtype)


def ladder_call(gathered, near, far, across, pair_labels, cols):
    count, width, _ = near.shape
    pairs = pair_labels.shape[0]
    group = 4
    depth, lanes = 2 * count * width, pairs * width
    vmem = pl.BlockSpec(memory_space=pltpu.VMEM)
    anywhere = pl.BlockSpec(memory_space=pl.ANY)
    close = functools.partial(pltpu.with_memory_space_constraint, memory_space=pltpu.VMEM)
    return pl.pallas_call(
        functools.partial(ladder_kernel, cols, group, 2 * LANES),
        out_shape=pltpu.VMEM(gathered.shape, jnp.bfloat16),
        in_specs=[vmem, vmem, vmem, anywhere, vmem],
        out_specs=vmem,
        scratch_shapes=[
            pltpu.VMEM((depth, lanes), jnp.bfloat16),
            pltpu.VMEM((lanes, width), jnp.bfloat16),
            pltpu.VMEM((width, lanes), jnp.float32),
            pltpu.VMEM((2 * count // group, width, group * width), jnp.bfloat16),
            pltpu.VMEM((count * width, width), jnp.bfloat16),
            pltpu.SemaphoreType.DMA(()),
        ],
        compiler_params=pltpu.CompilerParams(vmem_limit_bytes=40 * 2**20),
    )(
        close(jnp.broadcast_to(pair_labels[:, None], (pairs, LANES))),
        close(gathered),
        close(near.reshape(count * width, width)),
        pltpu.with_memory_space_constraint(far.reshape(count * width, width), pltpu.HBM),
        close(across),
    )


def body(amplitudes, factors, vir_irrep, pair_irrep):
    row_block, pairs_here, col_block = amplitudes.shape
    width = vir_irrep.shape[0]
    rows, cols = width // row_block, width // col_block
    held = pairs_here // CORES
    inner = held * col_block
    plane = ("col", "pair")
    core = lax.axis_index("row") % CORES
    swap = [(k, k ^ 1) for k in range(rows)]

    other_factors = lax.ppermute(factors, "row", swap)

    col_labels = lax.dynamic_slice_in_dim(vir_irrep, lax.axis_index("col") * col_block, col_block)
    pairs_held = lax.dynamic_slice_in_dim(pair_irrep, core * held, held)
    partner = jnp.bitwise_xor(pairs_held[:, None], col_labels[None, :]).reshape(1, inner)
    across = vir_irrep[None, :]

    sent = spread_call(amplitudes, rows)
    tall = lax.all_to_all(sent, "row", 0, 0, tiled=True)
    groups = cols * lax.axis_size("pair")
    block = fold_call(tall, across, partner, row_block, col_block, groups)
    block, late_vir, late_pair = lax.optimization_barrier((block, vir_irrep, pair_irrep))
    gathered = lax.all_to_all(block, plane, 0, 0, tiled=True)

    other_pairs = lax.ppermute(late_pair, "pair", [(0, 1), (1, 0)])
    first = lax.axis_index("pair") == 0
    pair_labels = jnp.stack(
        [jnp.where(first, late_pair, other_pairs), jnp.where(first, other_pairs, late_pair)]
    )
    pair_labels = lax.dynamic_slice_in_dim(pair_labels, core * held, held, axis=1).reshape(-1)
    row_labels = lax.dynamic_slice_in_dim(late_vir, lax.axis_index("row") * row_block, row_block)

    partial_sums = ladder_call(gathered, other_factors, factors, across, pair_labels, cols)

    pieces = lax.all_to_all(partial_sums, plane, 0, 0, tiled=True)
    packed = pack_call(pieces, rows, row_block, col_block)
    need = jnp.bitwise_xor(pair_irrep[:, None], col_labels[None, :]).reshape(CORES, inner)
    packed, row_labels, need = lax.optimization_barrier(
        (packed, jnp.broadcast_to(row_labels[:, None], (row_block, LANES)), need)
    )
    finals = lax.all_to_all(packed, "row", 0, 0, tiled=True)
    return unpack_call(finals, row_labels, need, amplitudes.shape)


def solution(mesh):
    placed = (P("row", "pair", "col"), P(("row", "col", "pair"), None, None), P(), P("pair"))
    return jax.shard_map(
        body, mesh=mesh, in_specs=placed, out_specs=P("row", "pair", "col"), check_vma=False
    )
```

```python
import functools

import jax
import jax.numpy as jnp
from jax import lax
from jax.experimental import pallas as pl
from jax.experimental.pallas import tpu as pltpu
from jax.sharding import PartitionSpec as P


LANES = 128
FOLD = 80
LEFT = LANES - FOLD
REST = FOLD - LEFT
SUB = 8
CORES = 2


def lanes():
    return lax.broadcasted_iota(jnp.int32, (1, LANES), 1)


def turn(x, shift):
    shift = shift % LANES
    return pltpu.roll(x, shift, 1) if shift else x


def join(first, second):
    lane = lanes()
    block = second.shape[0]
    main = jnp.where(lane < FOLD, first, turn(second, FOLD))
    rows, per_row = [], LANES // REST
    for start in range(0, block // SUB, per_row):
        row = jnp.zeros((SUB, LANES), jnp.float32)
        for k in range(min(per_row, block // SUB - start)):
            at = (start + k) * SUB
            moved = turn(second[at : at + SUB], k * REST - LEFT)
            row = jnp.where((lane >= k * REST) & (lane < (k + 1) * REST), moved, row)
        rows.append(row)
    return jnp.concatenate([main] + rows, axis=0)


def joined_rows(block):
    return block + -(-(block // SUB) // (LANES // REST)) * SUB


def part(x, block):
    lane = lanes()
    per_row = LANES // REST
    first = x[:block]
    tail = [
        turn(
            x[block + g // per_row * SUB : block + (g // per_row + 1) * SUB],
            LEFT - g % per_row * REST,
        )
        for g in range(block // SUB)
    ]
    second = jnp.where(lane < LEFT, turn(first, -FOLD), jnp.concatenate(tail, axis=0))
    return first, second


def fold(pieces):
    lane = lanes()
    total, by_shift = None, {}
    for t, piece in enumerate(pieces):
        base = t * LANES
        for m in range(base // FOLD, -(-(base + LANES) // FOLD)):
            low, high = max(m * FOLD - base, 0), min((m + 1) * FOLD - base, LANES)
            inside = jnp.where((lane >= low) & (lane < high), piece, 0.0)
            shift = (base - m * FOLD) % LANES
            by_shift[shift] = inside if shift not in by_shift else by_shift[shift] + inside
    for shift, piece in by_shift.items():
        moved = turn(piece, shift)
        total = moved if total is None else total + moved
    return total


PACK = 16


def spread_kernel(amp_ref, out_ref):
    row_block, pairs_here, col_block = amp_ref.shape
    held = pairs_here // CORES
    lines = held * col_block
    amp = amp_ref[...].astype(jnp.float32)
    for c in range(CORES):
        lane_side = jnp.concatenate([amp[:, c * held + j, :] for j in range(held)], axis=1)
        column = lane_side.T
        groups = [column[g * PACK : (g + 1) * PACK] for g in range(lines // PACK)]
        rest = LANES - row_block * len(groups)
        groups.append(jnp.zeros((PACK, rest), jnp.float32))
        packed = jnp.concatenate(groups, axis=1).astype(out_ref.dtype)
        for m in range(c, out_ref.shape[0], CORES):
            out_ref[m] = packed


def fold_kernel(row_block, tall_ref, across_ref, partner_ref, out_ref):
    groups, held, col_block, _ = out_ref.shape
    width = across_ref.shape[1]
    lines = held * col_block
    tiles = -(-width // LANES)
    filler = jnp.full((1, tiles * LANES - width), -1, jnp.int32)
    labels = jnp.concatenate([across_ref[...], filler], axis=1)
    partner = jnp.broadcast_to(partner_ref[...], (8, lines)).T[:, :1]
    lane = lax.broadcasted_iota(jnp.int32, (1, LANES), 1)
    folded = [jnp.zeros((PACK, LANES), jnp.float32) for _ in range(lines // PACK)]
    for r in range(tall_ref.shape[0]):
        tile, low = r * row_block // LANES, r * row_block % LANES
        here = jnp.where(
            (lane >= low) & (lane < low + row_block), labels[:, tile * LANES : (tile + 1) * LANES], -1
        )
        over = low + row_block - LANES
        if over > 0:
            following = labels[:, (tile + 1) * LANES : (tile + 2) * LANES]
            here = jnp.where(lane < over, following, here)
        piece = tall_ref[r].astype(jnp.float32)
        for g in range(lines // PACK):
            shift = (r - g) * row_block % LANES
            moved = pltpu.roll(piece, shift, 1) if shift else piece
            fits = partner[g * PACK : (g + 1) * PACK] == here
            folded[g] = folded[g] + jnp.where(fits, moved, 0.0)
    block = jnp.concatenate(folded, axis=0)
    for j in range(held):
        part = block[j * col_block : (j + 1) * col_block].astype(out_ref.dtype)
        for m in range(groups):
            out_ref[m, j] = part


def spread_call(amplitudes, rows):
    vmem = pl.BlockSpec(memory_space=pltpu.VMEM)
    return pl.pallas_call(
        spread_kernel,
        out_shape=jax.ShapeDtypeStruct((rows, PACK, LANES), amplitudes.dtype),
        in_specs=[vmem],
        out_specs=vmem,
        compiler_params=pltpu.CompilerParams(vmem_limit_bytes=8 * 2**20),
    )(amplitudes)


def fold_call(tall, across, partner, row_block, shape):
    vmem = pl.BlockSpec(memory_space=pltpu.VMEM)
    close = functools.partial(pltpu.with_memory_space_constraint, memory_space=pltpu.VMEM)
    return pl.pallas_call(
        functools.partial(fold_kernel, row_block),
        out_shape=jax.ShapeDtypeStruct(shape, tall.dtype),
        in_specs=[vmem] * 3,
        out_specs=vmem,
        compiler_params=pltpu.CompilerParams(vmem_limit_bytes=8 * 2**20),
    )(close(tall), close(across), close(partner))


def pack_kernel(row_block, col_block, pieces_ref, out_ref):
    total = pieces_ref[0].astype(jnp.float32)
    for m in range(1, pieces_ref.shape[0]):
        total = total + pieces_ref[m].astype(jnp.float32)
    total = jnp.concatenate(part(total, col_block), axis=0)
    lane = lanes()
    period = FOLD // row_block
    for k in range(period):
        packed = jnp.zeros((PACK, LANES), jnp.float32)
        for g in range(total.shape[0] // PACK):
            moved = turn(total[g * PACK : (g + 1) * PACK], (g - k) * row_block)
            packed = jnp.where(
                (lane >= g * row_block) & (lane < (g + 1) * row_block), moved, packed
            )
        for r in range(k, out_ref.shape[0], period):
            out_ref[r] = packed


def unpack_kernel(finals_ref, down_ref, across_ref, out_ref):
    row_block, pairs_here, col_block = out_ref.shape
    held = pairs_here // CORES
    lines = held * col_block
    for c in range(CORES):
        total = finals_ref[c]
        for z in range(CORES + c, finals_ref.shape[0], CORES):
            total = total + finals_ref[z]
        spread = jnp.concatenate(
            [
                turn(total, -g * row_block)
                for g in range(lines // PACK)
            ],
            axis=0,
        )
        spread = jnp.where(
            down_ref[:, :1] == across_ref[c : c + 1, :lines], spread.T[:row_block], 0.0
        )
        for j in range(held):
            out_ref[:, c * held + j, :] = spread[:, j * col_block : (j + 1) * col_block]


def pack_call(pieces, rows, row_block, col_block):
    close = functools.partial(pltpu.with_memory_space_constraint, memory_space=pltpu.VMEM)
    vmem = pl.BlockSpec(memory_space=pltpu.VMEM)
    return pl.pallas_call(
        functools.partial(pack_kernel, row_block, col_block),
        out_shape=jax.ShapeDtypeStruct((rows, PACK, LANES), jnp.float32),
        in_specs=[vmem],
        out_specs=vmem,
        compiler_params=pltpu.CompilerParams(vmem_limit_bytes=8 * 2**20),
    )(close(pieces))


def unpack_call(finals, down, across, shape):
    close = functools.partial(pltpu.with_memory_space_constraint, memory_space=pltpu.VMEM)
    vmem = pl.BlockSpec(memory_space=pltpu.VMEM)
    return pl.pallas_call(
        unpack_kernel,
        out_shape=jax.ShapeDtypeStruct(shape, jnp.float32),
        in_specs=[vmem] * 3,
        out_specs=vmem,
        compiler_params=pltpu.CompilerParams(vmem_limit_bytes=8 * 2**20),
    )(close(finals), close(down), close(across))


def ladder_kernel(
    cols,
    group,
    lane_group,
    pair_ref,
    t_ref,
    near_ref,
    far_ref,
    across_ref,
    out_ref,
    inner,
    amp,
    ladders,
    side,
    stack,
    arrived,
):
    width = across_ref.shape[1]
    half_depth = near_ref.shape[0]
    groups, pairs = t_ref.shape[0] // cols, pair_ref.shape[0]
    tiles = -(-width // LANES)
    block = width // cols
    step = group * width
    half_steps = half_depth // step

    fetch = pltpu.make_async_copy(far_ref, stack, arrived)
    fetch.start()
    filler = jnp.full((1, tiles * LANES - width), -1, jnp.int32)
    down = jnp.broadcast_to(across_ref[...], (8, width)).T[:, :1]
    mixed = jnp.bitwise_xor(down, jnp.concatenate([across_ref[...], filler], axis=1))
    for p in range(pairs):
        half, at = p // CORES, p % CORES
        rows = jnp.concatenate(
            [t_ref[q * groups + half, at].astype(jnp.float32) for q in range(cols)], axis=0
        )
        spread = jnp.where(mixed == pair_ref[p : p + 1, :1], jnp.concatenate([rows] * tiles, axis=1), 0.0)
        amp[p * width : (p + 1) * width, :] = spread.astype(jnp.bfloat16)[:, :width]

    for source, base in ((near_ref, 0), (stack, half_steps)):
        if base:
            fetch.wait()

        @pl.loop(0, half_steps)
        def _(g, source=source, base=base):
            here = pl.multiple_of(g * step, step)
            there = pl.multiple_of((base + g) * step, step)
            for k in range(group):
                side[base + g, :, k * width : (k + 1) * width] = source[
                    pl.ds(pl.multiple_of(here + k * width, width), width), :
                ]
            part = lax.dot_general(
                amp[...],
                source[pl.ds(here, step), :],
                (((1,), (1,)), ((), ())),
                preferred_element_type=jnp.float32,
            ).astype(jnp.bfloat16)
            for p in range(pairs):
                for k in range(group):
                    inner[
                        pl.ds(pl.multiple_of(there + k * width, width), width),
                        p * width : (p + 1) * width,
                    ] = part[p * width : (p + 1) * width, k * width : (k + 1) * width]

    for start in range(0, pairs * width, lane_group):
        lanes = slice(start, start + lane_group)
        total = None
        for g in range(2 * half_steps):
            term = jnp.dot(
                side[g], inner[g * step : (g + 1) * step, lanes], preferred_element_type=jnp.float32
            )
            total = term if total is None else total + term
        ladders[:, lanes] = total

    blank = jnp.zeros((width, tiles * LANES - width), jnp.float32)
    for half in range(groups):
        both = []
        for at in range(CORES):
            p = half * CORES + at
            ladder = jnp.concatenate([ladders[:, p * width : (p + 1) * width], blank], axis=1)
            ladder = jnp.where(mixed == pair_ref[p : p + 1, :1], ladder, 0.0)
            tall = ladder[:FOLD]
            for start in range(FOLD, width, FOLD):
                tall = tall + ladder[start : start + FOLD]
            tall = jnp.concatenate(
                [tall, jnp.zeros((LANES - FOLD, tiles * LANES), jnp.float32)], axis=0
            )
            flat = fold([ladder[:, t * LANES : (t + 1) * LANES] for t in range(tiles)])
            both.append(flat + tall.T[:width])
        for q in range(cols):
            span = slice(q * block, (q + 1) * block)
            out_ref[q * groups + half] = join(both[0][span], both[1][span]).astype(out_ref.dtype)


def ladder_call(gathered, near, far, across, pair_labels, cols):
    count, width, _ = near.shape
    pairs = pair_labels.shape[0]
    group = 4
    depth, lanes = 2 * count * width, pairs * width
    vmem = pl.BlockSpec(memory_space=pltpu.VMEM)
    anywhere = pl.BlockSpec(memory_space=pl.ANY)
    close = functools.partial(pltpu.with_memory_space_constraint, memory_space=pltpu.VMEM)
    return pl.pallas_call(
        functools.partial(ladder_kernel, cols, group, 2 * LANES),
        out_shape=jax.ShapeDtypeStruct(
            (gathered.shape[0], joined_rows(width // cols), LANES), jnp.bfloat16
        ),
        in_specs=[vmem, vmem, vmem, anywhere, vmem],
        out_specs=vmem,
        scratch_shapes=[
            pltpu.VMEM((depth, lanes), jnp.bfloat16),
            pltpu.VMEM((lanes, width), jnp.bfloat16),
            pltpu.VMEM((width, lanes), jnp.float32),
            pltpu.VMEM((2 * count // group, width, group * width), jnp.bfloat16),
            pltpu.VMEM((count * width, width), jnp.bfloat16),
            pltpu.SemaphoreType.DMA(()),
        ],
        compiler_params=pltpu.CompilerParams(vmem_limit_bytes=40 * 2**20),
    )(
        close(jnp.broadcast_to(pair_labels[:, None], (pairs, LANES))),
        close(gathered),
        close(near.reshape(count * width, width)),
        pltpu.with_memory_space_constraint(far.reshape(count * width, width), pltpu.HBM),
        close(across),
    )


def body(amplitudes, factors, vir_irrep, pair_irrep):
    row_block, pairs_here, col_block = amplitudes.shape
    width = vir_irrep.shape[0]
    rows, cols = width // row_block, width // col_block
    held = pairs_here // CORES
    inner = held * col_block
    plane = ("col", "pair")
    core = lax.axis_index("row") % CORES
    swap = [(k, k ^ 1) for k in range(rows)]

    other_factors = lax.ppermute(factors, "row", swap)

    col_labels = lax.dynamic_slice_in_dim(vir_irrep, lax.axis_index("col") * col_block, col_block)
    pairs_held = lax.dynamic_slice_in_dim(pair_irrep, core * held, held)
    partner = jnp.bitwise_xor(pairs_held[:, None], col_labels[None, :]).reshape(1, inner)
    across = vir_irrep[None, :]

    sent = spread_call(amplitudes, rows)
    tall = lax.all_to_all(sent, "row", 0, 0, tiled=True)
    groups = cols * lax.axis_size("pair")
    block = fold_call(tall, across, partner, row_block, (groups, held, col_block, LANES))
    block, late_vir, late_pair = lax.optimization_barrier((block, vir_irrep, pair_irrep))
    gathered = lax.all_to_all(block, plane, 0, 0, tiled=True)

    other_pairs = lax.ppermute(late_pair, "pair", [(0, 1), (1, 0)])
    first = lax.axis_index("pair") == 0
    pair_labels = jnp.stack(
        [jnp.where(first, late_pair, other_pairs), jnp.where(first, other_pairs, late_pair)]
    )
    pair_labels = lax.dynamic_slice_in_dim(pair_labels, core * held, held, axis=1).reshape(-1)
    row_labels = lax.dynamic_slice_in_dim(late_vir, lax.axis_index("row") * row_block, row_block)

    partial_sums = ladder_call(gathered, other_factors, factors, across, pair_labels, cols)

    pieces = lax.all_to_all(partial_sums, plane, 0, 0, tiled=True)
    packed = pack_call(pieces, rows, row_block, col_block)
    need = jnp.bitwise_xor(late_pair[:, None], col_labels[None, :]).reshape(CORES, inner)
    packed, row_labels, need = lax.optimization_barrier(
        (packed, jnp.broadcast_to(row_labels[:, None], (row_block, LANES)), need)
    )
    finals = lax.all_to_all(packed, "row", 0, 0, tiled=True)
    return unpack_call(finals, row_labels, need, amplitudes.shape)


def solution(mesh):
    placed = (P("row", "pair", "col"), P(("row", "col", "pair"), None, None), P(), P("pair"))
    return jax.shard_map(
        body, mesh=mesh, in_specs=placed, out_specs=P("row", "pair", "col"), check_vma=False
    )
```

```python
import functools

import jax
import jax.numpy as jnp
from jax import lax
from jax.experimental import pallas as pl
from jax.experimental.pallas import tpu as pltpu
from jax.sharding import PartitionSpec as P


LANES = 128
FOLD = 80
LEFT = LANES - FOLD
REST = FOLD - LEFT
SUB = 8
CORES = 2


def lanes():
    return lax.broadcasted_iota(jnp.int32, (1, LANES), 1)


def turn(x, shift):
    shift = shift % LANES
    return pltpu.roll(x, shift, 1) if shift else x


def join(first, second):
    lane = lanes()
    block = second.shape[0]
    main = jnp.where(lane < FOLD, first, turn(second, FOLD))
    rows, per_row = [], LANES // REST
    for start in range(0, block // SUB, per_row):
        row = jnp.zeros((SUB, LANES), jnp.float32)
        for k in range(min(per_row, block // SUB - start)):
            at = (start + k) * SUB
            moved = turn(second[at : at + SUB], k * REST - LEFT)
            row = jnp.where((lane >= k * REST) & (lane < (k + 1) * REST), moved, row)
        rows.append(row)
    return jnp.concatenate([main] + rows, axis=0)


def joined_rows(block):
    return block + -(-(block // SUB) // (LANES // REST)) * SUB


def part(x, block):
    lane = lanes()
    per_row = LANES // REST
    first = x[:block]
    tail = [
        turn(
            x[block + g // per_row * SUB : block + (g // per_row + 1) * SUB],
            LEFT - g % per_row * REST,
        )
        for g in range(block // SUB)
    ]
    second = jnp.where(lane < LEFT, turn(first, -FOLD), jnp.concatenate(tail, axis=0))
    return first, second


def unfold(x, tiles):
    lane = lanes()
    out = []
    for t in range(tiles):
        base = t * LANES
        tile = None
        for m in range(base // FOLD, -(-(base + LANES) // FOLD)):
            moved = turn(x, m * FOLD - base)
            tile = moved if tile is None else jnp.where(lane >= m * FOLD - base, moved, tile)
        out.append(tile)
    return out


def fold(pieces):
    lane = lanes()
    total, by_shift = None, {}
    for t, piece in enumerate(pieces):
        base = t * LANES
        for m in range(base // FOLD, -(-(base + LANES) // FOLD)):
            low, high = max(m * FOLD - base, 0), min((m + 1) * FOLD - base, LANES)
            inside = jnp.where((lane >= low) & (lane < high), piece, 0.0)
            shift = (base - m * FOLD) % LANES
            by_shift[shift] = inside if shift not in by_shift else by_shift[shift] + inside
    for shift, piece in by_shift.items():
        moved = turn(piece, shift)
        total = moved if total is None else total + moved
    return total


PACK = 16


def pick(row, index, size):
    out = row[:, :size]
    for k in range(1, row.shape[1] // size):
        out = jnp.where(index == k, row[:, k * size : (k + 1) * size], out)
    return out


def split_labels(label_ref, width):
    return label_ref[:, :width], label_ref[:, width:]


def as_column(row):
    return jnp.broadcast_to(row, (SUB, row.shape[1])).T[:, :1]


def spread_kernel(amp_ref, out_ref):
    row_block, pairs_here, col_block = amp_ref.shape
    held = pairs_here // CORES
    lines = held * col_block
    amp = amp_ref[...].astype(jnp.float32)
    for c in range(CORES):
        lane_side = jnp.concatenate([amp[:, c * held + j, :] for j in range(held)], axis=1)
        column = lane_side.T
        groups = [column[g * PACK : (g + 1) * PACK] for g in range(lines // PACK)]
        rest = LANES - row_block * len(groups)
        groups.append(jnp.zeros((PACK, rest), jnp.float32))
        packed = jnp.concatenate(groups, axis=1).astype(out_ref.dtype)
        for m in range(c, out_ref.shape[0], CORES):
            out_ref[m] = packed


def fold_kernel(row_block, col_block, tall_ref, label_ref, out_ref):
    width = tall_ref.shape[0] * row_block
    across, own_pairs = split_labels(label_ref, width)
    held = own_pairs.shape[1] // CORES
    lines = held * col_block
    mine = pick(across, lax.axis_index("col"), col_block)
    pairs = pick(own_pairs, lax.axis_index("row") % CORES, held)
    partner = as_column(
        jnp.concatenate([jnp.bitwise_xor(mine, pairs[:, j : j + 1]) for j in range(held)], axis=1)
    )
    lane = lanes()
    filler = jnp.full((1, LANES - FOLD), -1, jnp.int32)
    folded = [jnp.zeros((PACK, LANES), jnp.float32) for _ in range(lines // PACK)]
    for m in range(width // FOLD):
        labels = jnp.concatenate([across[:, m * FOLD : (m + 1) * FOLD], filler], axis=1)
        for k in range(FOLD // row_block):
            low = k * row_block
            here = jnp.where((lane >= low) & (lane < low + row_block), labels, -1)
            piece = tall_ref[m * (FOLD // row_block) + k].astype(jnp.float32)
            for g in range(lines // PACK):
                fits = partner[g * PACK : (g + 1) * PACK] == here
                folded[g] = folded[g] + jnp.where(fits, turn(piece, (k - g) * row_block), 0.0)
    block = jnp.concatenate(folded, axis=0)
    block = join(block[:col_block], block[col_block:]).astype(out_ref.dtype)
    for m in range(out_ref.shape[0]):
        out_ref[m] = block


def spread_call(amplitudes, rows):
    vmem = pl.BlockSpec(memory_space=pltpu.VMEM)
    return pl.pallas_call(
        spread_kernel,
        out_shape=jax.ShapeDtypeStruct((rows, PACK, LANES), amplitudes.dtype),
        in_specs=[vmem],
        out_specs=vmem,
        compiler_params=pltpu.CompilerParams(vmem_limit_bytes=8 * 2**20),
    )(amplitudes)


def fold_call(tall, labels, row_block, col_block, groups):
    vmem = pl.BlockSpec(memory_space=pltpu.VMEM)
    close = functools.partial(pltpu.with_memory_space_constraint, memory_space=pltpu.VMEM)
    return pl.pallas_call(
        functools.partial(fold_kernel, row_block, col_block),
        out_shape=jax.ShapeDtypeStruct((groups, joined_rows(col_block), LANES), tall.dtype),
        in_specs=[vmem] * 2,
        out_specs=vmem,
        compiler_params=pltpu.CompilerParams(vmem_limit_bytes=8 * 2**20),
    )(close(tall), close(labels))


def pack_kernel(row_block, col_block, pieces_ref, out_ref):
    total = pieces_ref[0].astype(jnp.float32)
    for m in range(1, pieces_ref.shape[0]):
        total = total + pieces_ref[m].astype(jnp.float32)
    total = jnp.concatenate(part(total, col_block), axis=0)
    lane = lanes()
    period = FOLD // row_block
    for k in range(period):
        packed = jnp.zeros((PACK, LANES), jnp.float32)
        for g in range(total.shape[0] // PACK):
            moved = turn(total[g * PACK : (g + 1) * PACK], (g - k) * row_block)
            packed = jnp.where(
                (lane >= g * row_block) & (lane < (g + 1) * row_block), moved, packed
            )
        for r in range(k, out_ref.shape[0], period):
            out_ref[r] = packed


def unpack_kernel(finals_ref, label_ref, out_ref):
    row_block, pairs_here, col_block = out_ref.shape
    held = pairs_here // CORES
    lines = held * col_block
    width = finals_ref.shape[0] * row_block
    across, own_pairs = split_labels(label_ref, width)
    down = as_column(pick(across, lax.axis_index("row"), row_block))
    mine = pick(across, lax.axis_index("col"), col_block)
    for c in range(CORES):
        total = finals_ref[c]
        for z in range(CORES + c, finals_ref.shape[0], CORES):
            total = total + finals_ref[z]
        spread = jnp.concatenate(
            [
                turn(total, -g * row_block)
                for g in range(lines // PACK)
            ],
            axis=0,
        )
        spread = spread.T[:row_block]
        for j in range(held):
            at = c * held + j
            wanted = jnp.bitwise_xor(mine, own_pairs[:, at : at + 1])
            piece = spread[:, j * col_block : (j + 1) * col_block]
            out_ref[:, at, :] = jnp.where(down == wanted, piece, 0.0)


def pack_call(pieces, rows, row_block, col_block):
    close = functools.partial(pltpu.with_memory_space_constraint, memory_space=pltpu.VMEM)
    vmem = pl.BlockSpec(memory_space=pltpu.VMEM)
    return pl.pallas_call(
        functools.partial(pack_kernel, row_block, col_block),
        out_shape=jax.ShapeDtypeStruct((rows, PACK, LANES), jnp.float32),
        in_specs=[vmem],
        out_specs=vmem,
        compiler_params=pltpu.CompilerParams(vmem_limit_bytes=8 * 2**20),
    )(close(pieces))


def unpack_call(finals, labels, shape):
    close = functools.partial(pltpu.with_memory_space_constraint, memory_space=pltpu.VMEM)
    vmem = pl.BlockSpec(memory_space=pltpu.VMEM)
    return pl.pallas_call(
        unpack_kernel,
        out_shape=jax.ShapeDtypeStruct(shape, jnp.float32),
        in_specs=[vmem] * 2,
        out_specs=vmem,
        compiler_params=pltpu.CompilerParams(vmem_limit_bytes=8 * 2**20),
    )(close(finals), close(labels))


def ladder_kernel(
    cols,
    group,
    lane_group,
    other_pair_ref,
    t_ref,
    near_ref,
    far_ref,
    label_ref,
    out_ref,
    inner,
    amp,
    ladders,
    side,
    stack,
    arrived,
):
    half_depth, width = near_ref.shape
    across, own_pairs = split_labels(label_ref, width)
    groups = t_ref.shape[0] // cols
    pairs = own_pairs.shape[1] // CORES * groups
    tiles = -(-width // LANES)
    block = width // cols
    step = group * width
    half_steps = half_depth // step

    fetch = pltpu.make_async_copy(far_ref, stack, arrived)
    fetch.start()
    filler = jnp.full((1, tiles * LANES - width), -1, jnp.int32)
    down = as_column(across)
    mixed = jnp.bitwise_xor(down, jnp.concatenate([across, filler], axis=1))
    core, place = lax.axis_index("row") % CORES, lax.axis_index("pair")
    own_pairs = pick(own_pairs, core, pairs // groups)
    other_pairs = pick(other_pair_ref[...], core, pairs // groups)
    wanted = []
    for half in range(groups):
        chosen = jnp.where(place == half, own_pairs, other_pairs)
        wanted += [chosen[:, j : j + 1] for j in range(pairs // groups)]
    for half in range(groups):
        both = [part(t_ref[q * groups + half].astype(jnp.float32), block) for q in range(cols)]
        for at in range(CORES):
            p = half * CORES + at
            rows = jnp.concatenate([pieces[at] for pieces in both], axis=0)
            spread = jnp.concatenate(unfold(rows, tiles), axis=1)
            spread = jnp.where(mixed == wanted[p], spread, 0.0)
            amp[p * width : (p + 1) * width, :] = spread.astype(jnp.bfloat16)[:, :width]

    for source, base in ((near_ref, 0), (stack, half_steps)):
        if base:
            fetch.wait()

        @pl.loop(0, half_steps)
        def _(g, source=source, base=base):
            here = pl.multiple_of(g * step, step)
            there = pl.multiple_of((base + g) * step, step)
            for k in range(group):
                side[base + g, :, k * width : (k + 1) * width] = source[
                    pl.ds(pl.multiple_of(here + k * width, width), width), :
                ]
            part = lax.dot_general(
                amp[...],
                source[pl.ds(here, step), :],
                (((1,), (1,)), ((), ())),
                preferred_element_type=jnp.float32,
            ).astype(jnp.bfloat16)
            for p in range(pairs):
                for k in range(group):
                    inner[
                        pl.ds(pl.multiple_of(there + k * width, width), width),
                        p * width : (p + 1) * width,
                    ] = part[p * width : (p + 1) * width, k * width : (k + 1) * width]

    for start in range(0, pairs * width, lane_group):
        lanes = slice(start, start + lane_group)
        total = None
        for g in range(2 * half_steps):
            term = jnp.dot(
                side[g], inner[g * step : (g + 1) * step, lanes], preferred_element_type=jnp.float32
            )
            total = term if total is None else total + term
        ladders[:, lanes] = total

    blank = jnp.zeros((width, tiles * LANES - width), jnp.float32)
    for half in range(groups):
        both = []
        for at in range(CORES):
            p = half * CORES + at
            ladder = jnp.concatenate([ladders[:, p * width : (p + 1) * width], blank], axis=1)
            ladder = jnp.where(mixed == wanted[p], ladder, 0.0)
            tall = ladder[:FOLD]
            for start in range(FOLD, width, FOLD):
                tall = tall + ladder[start : start + FOLD]
            tall = jnp.concatenate(
                [tall, jnp.zeros((LANES - FOLD, tiles * LANES), jnp.float32)], axis=0
            )
            flat = fold([ladder[:, t * LANES : (t + 1) * LANES] for t in range(tiles)])
            both.append(flat + tall.T[:width])
        for q in range(cols):
            span = slice(q * block, (q + 1) * block)
            out_ref[q * groups + half] = join(both[0][span], both[1][span]).astype(out_ref.dtype)


def ladder_call(gathered, near, far, labels, other_pairs, cols):
    count, width, _ = near.shape
    pairs = other_pairs.shape[1]
    group = 4
    depth, lanes = 2 * count * width, pairs * width
    vmem = pl.BlockSpec(memory_space=pltpu.VMEM)
    anywhere = pl.BlockSpec(memory_space=pl.ANY)
    close = functools.partial(pltpu.with_memory_space_constraint, memory_space=pltpu.VMEM)
    return pl.pallas_call(
        functools.partial(ladder_kernel, cols, group, 2 * LANES),
        out_shape=pltpu.VMEM(gathered.shape, jnp.bfloat16),
        in_specs=[vmem, vmem, vmem, anywhere, vmem],
        out_specs=vmem,
        scratch_shapes=[
            pltpu.VMEM((depth, lanes), jnp.bfloat16),
            pltpu.VMEM((lanes, width), jnp.bfloat16),
            pltpu.VMEM((width, lanes), jnp.float32),
            pltpu.VMEM((2 * count // group, width, group * width), jnp.bfloat16),
            pltpu.VMEM((count * width, width), jnp.bfloat16),
            pltpu.SemaphoreType.DMA(()),
        ],
        compiler_params=pltpu.CompilerParams(vmem_limit_bytes=40 * 2**20),
    )(
        close(other_pairs),
        close(gathered),
        close(near.reshape(count * width, width)),
        pltpu.with_memory_space_constraint(far.reshape(count * width, width), pltpu.HBM),
        close(labels),
    )


def body(amplitudes, factors, vir_irrep, pair_irrep):
    row_block, _, col_block = amplitudes.shape
    width = vir_irrep.shape[0]
    rows, cols = width // row_block, width // col_block
    plane = ("col", "pair")
    swap = [(k, k ^ 1) for k in range(rows)]
    labels = jnp.concatenate([vir_irrep, pair_irrep])[None, :]

    other_factors = lax.ppermute(factors, "row", swap)
    other_pairs = lax.ppermute(pair_irrep[None, :], "pair", [(0, 1), (1, 0)])

    sent = spread_call(amplitudes, rows)
    tall = lax.all_to_all(sent, "row", 0, 0, tiled=True)
    tall, other_pairs = lax.optimization_barrier((tall, other_pairs))
    groups = cols * lax.axis_size("pair")
    block = fold_call(tall, labels, row_block, col_block, groups)
    gathered = lax.all_to_all(block, plane, 0, 0, tiled=True)
    partial_sums = ladder_call(gathered, other_factors, factors, labels, other_pairs, cols)
    pieces = lax.all_to_all(partial_sums, plane, 0, 0, tiled=True)
    packed = pack_call(pieces, rows, row_block, col_block)
    finals = lax.all_to_all(packed, "row", 0, 0, tiled=True)
    return unpack_call(finals, labels, amplitudes.shape)


def solution(mesh):
    placed = (P("row", "pair", "col"), P(("row", "col", "pair"), None, None), P(), P("pair"))
    return jax.shard_map(
        body, mesh=mesh, in_specs=placed, out_specs=P("row", "pair", "col"), check_vma=False
    )
```

```python
import functools

import jax
import jax.numpy as jnp
from jax import lax
from jax.experimental import pallas as pl
from jax.experimental.pallas import tpu as pltpu
from jax.sharding import PartitionSpec as P


LANES = 128
FOLD = 80
LEFT = LANES - FOLD
REST = FOLD - LEFT
SUB = 8
TAG = LANES - 2
CORES = 2


def lanes():
    return lax.broadcasted_iota(jnp.int32, (1, LANES), 1)


def turn(x, shift):
    shift = shift % LANES
    return pltpu.roll(x, shift, 1) if shift else x


def join(first, second):
    lane = lanes()
    block = second.shape[0]
    main = jnp.where(lane < FOLD, first, turn(second, FOLD))
    rows, per_row = [], LANES // REST
    for start in range(0, block // SUB, per_row):
        row = jnp.zeros((SUB, LANES), jnp.float32)
        for k in range(min(per_row, block // SUB - start)):
            at = (start + k) * SUB
            moved = turn(second[at : at + SUB], k * REST - LEFT)
            row = jnp.where((lane >= k * REST) & (lane < (k + 1) * REST), moved, row)
        rows.append(row)
    return jnp.concatenate([main] + rows, axis=0)


def joined_rows(block):
    return block + -(-(block // SUB) // (LANES // REST)) * SUB


def part(x, block):
    lane = lanes()
    per_row = LANES // REST
    first = x[:block]
    tail = [
        turn(
            x[block + g // per_row * SUB : block + (g // per_row + 1) * SUB],
            LEFT - g % per_row * REST,
        )
        for g in range(block // SUB)
    ]
    second = jnp.where(lane < LEFT, turn(first, -FOLD), jnp.concatenate(tail, axis=0))
    return first, second


def spreader(columns):
    down = lax.broadcasted_iota(jnp.int32, (LANES, columns), 0)
    across = lax.broadcasted_iota(jnp.int32, (LANES, columns), 1)
    hit = down == across
    for m in range(1, -(-columns // FOLD)):
        hit = hit | (down == across - m * FOLD)
    return jnp.where(hit & (down < FOLD), 1.0, 0.0).astype(jnp.bfloat16)


def fold(pieces):
    lane = lanes()
    total, by_shift = None, {}
    for t, piece in enumerate(pieces):
        base = t * LANES
        for m in range(base // FOLD, -(-(base + LANES) // FOLD)):
            low, high = max(m * FOLD - base, 0), min((m + 1) * FOLD - base, LANES)
            inside = jnp.where((lane >= low) & (lane < high), piece, 0.0)
            shift = (base - m * FOLD) % LANES
            by_shift[shift] = inside if shift not in by_shift else by_shift[shift] + inside
    for shift, piece in by_shift.items():
        moved = turn(piece, shift)
        total = moved if total is None else total + moved
    return total


PACK = 16


def pick(row, index, size):
    out = row[:, :size]
    for k in range(1, row.shape[1] // size):
        out = jnp.where(index == k, row[:, k * size : (k + 1) * size], out)
    return out


def split_labels(label_ref, width):
    return label_ref[:, :width], label_ref[:, width:]


def as_column(row):
    return jnp.broadcast_to(row, (SUB, row.shape[1])).T[:, :1]


def spread_kernel(amp_ref, out_ref):
    row_block, pairs_here, col_block = amp_ref.shape
    held = pairs_here // CORES
    lines = held * col_block
    amp = amp_ref[...].astype(jnp.float32)
    for c in range(CORES):
        lane_side = jnp.concatenate([amp[:, c * held + j, :] for j in range(held)], axis=1)
        column = lane_side.T
        groups = [column[g * PACK : (g + 1) * PACK] for g in range(lines // PACK)]
        rest = LANES - row_block * len(groups)
        groups.append(jnp.zeros((PACK, rest), jnp.float32))
        packed = jnp.concatenate(groups, axis=1).astype(out_ref.dtype)
        for m in range(c, out_ref.shape[0], CORES):
            out_ref[m] = packed


def mask_kernel(width, label_ref, allowed_ref, partner_ref, tag_ref):
    pairs_here, row_block, col_block = allowed_ref.shape
    across, own_pairs = split_labels(label_ref, width)
    held = pairs_here // CORES
    down = as_column(pick(across, lax.axis_index("row"), row_block))
    mine = pick(across, lax.axis_index("col"), col_block)
    for at in range(pairs_here):
        wanted = jnp.bitwise_xor(mine, own_pairs[:, at : at + 1])
        allowed_ref[at] = jnp.where(down == wanted, 1, 0)
    pairs = pick(own_pairs, lax.axis_index("row") % CORES, held)
    partner = as_column(
        jnp.concatenate([jnp.bitwise_xor(mine, pairs[:, j : j + 1]) for j in range(held)], axis=1)
    )
    partner_ref[...] = jnp.broadcast_to(partner, partner_ref.shape)
    lane = lanes()
    tags = jnp.zeros((1, LANES), jnp.float32)
    for j in range(held):
        tags = jnp.where(lane == TAG + j, pairs[:, j : j + 1].astype(jnp.float32), tags)
    tag_ref[...] = jnp.broadcast_to(tags, tag_ref.shape)


def mask_call(labels, width, row_block, pairs_here, col_block):
    vmem = pl.BlockSpec(memory_space=pltpu.VMEM)
    lines = pairs_here // CORES * col_block
    return pl.pallas_call(
        functools.partial(mask_kernel, width),
        out_shape=(
            jax.ShapeDtypeStruct((pairs_here, row_block, col_block), jnp.int32),
            jax.ShapeDtypeStruct((lines, LANES), jnp.int32),
            jax.ShapeDtypeStruct((SUB, LANES), jnp.float32),
        ),
        in_specs=[vmem],
        out_specs=(vmem, vmem, vmem),
        compiler_params=pltpu.CompilerParams(vmem_limit_bytes=8 * 2**20),
    )(pltpu.with_memory_space_constraint(labels, pltpu.VMEM))


def fold_kernel(row_block, col_block, tall_ref, label_ref, partner_ref, tag_ref, out_ref):
    width = tall_ref.shape[0] * row_block
    across, _ = split_labels(label_ref, width)
    lines = partner_ref.shape[0]
    partner = partner_ref[...]
    lane = lanes()
    filler = jnp.full((1, LANES - FOLD), -1, jnp.int32)
    folded = [jnp.zeros((PACK, LANES), jnp.float32) for _ in range(lines // PACK)]
    for m in range(width // FOLD):
        labels = jnp.concatenate([across[:, m * FOLD : (m + 1) * FOLD], filler], axis=1)
        for k in range(FOLD // row_block):
            low = k * row_block
            here = jnp.where((lane >= low) & (lane < low + row_block), labels, -1)
            piece = tall_ref[m * (FOLD // row_block) + k].astype(jnp.float32)
            for g in range(lines // PACK):
                fits = partner[g * PACK : (g + 1) * PACK] == here
                folded[g] = folded[g] + jnp.where(fits, turn(piece, (k - g) * row_block), 0.0)
    block = jnp.concatenate(folded, axis=0)
    block = join(block[:col_block], block[col_block:])
    block = jnp.concatenate([block[:-SUB], block[-SUB:] + tag_ref[...]], axis=0)
    block = block.astype(out_ref.dtype)
    for m in range(out_ref.shape[0]):
        out_ref[m] = block


def spread_call(amplitudes, rows):
    vmem = pl.BlockSpec(memory_space=pltpu.VMEM)
    return pl.pallas_call(
        spread_kernel,
        out_shape=jax.ShapeDtypeStruct((rows, PACK, LANES), amplitudes.dtype),
        in_specs=[vmem],
        out_specs=vmem,
        compiler_params=pltpu.CompilerParams(vmem_limit_bytes=8 * 2**20),
    )(pltpu.with_memory_space_constraint(amplitudes, pltpu.HBM))


def fold_call(tall, labels, partner, tags, row_block, col_block, groups):
    vmem = pl.BlockSpec(memory_space=pltpu.VMEM)
    close = functools.partial(pltpu.with_memory_space_constraint, memory_space=pltpu.VMEM)
    return pl.pallas_call(
        functools.partial(fold_kernel, row_block, col_block),
        out_shape=jax.ShapeDtypeStruct((groups, joined_rows(col_block), LANES), tall.dtype),
        in_specs=[vmem] * 4,
        out_specs=vmem,
        compiler_params=pltpu.CompilerParams(vmem_limit_bytes=8 * 2**20),
    )(close(tall), close(labels), close(partner), close(tags))


def pack_kernel(row_block, col_block, pieces_ref, out_ref):
    total = pieces_ref[0].astype(jnp.float32)
    for m in range(1, pieces_ref.shape[0]):
        total = total + pieces_ref[m].astype(jnp.float32)
    total = jnp.concatenate(part(total, col_block), axis=0)
    lane = lanes()
    period = FOLD // row_block
    for k in range(period):
        packed = jnp.zeros((PACK, LANES), jnp.float32)
        for g in range(total.shape[0] // PACK):
            moved = turn(total[g * PACK : (g + 1) * PACK], (g - k) * row_block)
            packed = jnp.where(
                (lane >= g * row_block) & (lane < (g + 1) * row_block), moved, packed
            )
        for r in range(k, out_ref.shape[0], period):
            out_ref[r] = packed


def unpack_kernel(finals_ref, allowed_ref, out_ref):
    row_block, pairs_here, col_block = out_ref.shape
    held = pairs_here // CORES
    lines = held * col_block
    for c in range(CORES):
        total = finals_ref[c]
        for z in range(CORES + c, finals_ref.shape[0], CORES):
            total = total + finals_ref[z]
        spread = jnp.concatenate(
            [
                turn(total, -g * row_block)
                for g in range(lines // PACK)
            ],
            axis=0,
        )
        spread = spread.T[:row_block]
        for j in range(held):
            at = c * held + j
            piece = spread[:, j * col_block : (j + 1) * col_block]
            out_ref[:, at, :] = jnp.where(allowed_ref[at] != 0, piece, 0.0)


def pack_call(pieces, rows, row_block, col_block):
    close = functools.partial(pltpu.with_memory_space_constraint, memory_space=pltpu.VMEM)
    vmem = pl.BlockSpec(memory_space=pltpu.VMEM)
    return pl.pallas_call(
        functools.partial(pack_kernel, row_block, col_block),
        out_shape=jax.ShapeDtypeStruct((rows, PACK, LANES), jnp.float32),
        in_specs=[vmem],
        out_specs=vmem,
        compiler_params=pltpu.CompilerParams(vmem_limit_bytes=8 * 2**20),
    )(close(pieces))


def unpack_call(finals, allowed, shape):
    close = functools.partial(pltpu.with_memory_space_constraint, memory_space=pltpu.VMEM)
    vmem = pl.BlockSpec(memory_space=pltpu.VMEM)
    return pl.pallas_call(
        unpack_kernel,
        out_shape=jax.ShapeDtypeStruct(shape, jnp.float32),
        in_specs=[vmem] * 2,
        out_specs=vmem,
        compiler_params=pltpu.CompilerParams(vmem_limit_bytes=8 * 2**20),
    )(close(finals), close(allowed))


def ladder_kernel(
    cols,
    group,
    lane_group,
    t_ref,
    near_ref,
    far_ref,
    label_ref,
    out_ref,
    inner,
    amp,
    ladders,
    side,
    stack,
    arrived,
):
    half_depth, width = near_ref.shape
    across, own_pairs = split_labels(label_ref, width)
    groups = t_ref.shape[0] // cols
    held = own_pairs.shape[1] // CORES
    pairs = held * groups
    tiles = -(-width // LANES)
    block = width // cols
    step = group * width
    half_steps = half_depth // step

    fetch = pltpu.make_async_copy(far_ref, stack, arrived)
    fetch.start()
    filler = jnp.full((1, tiles * LANES - width), -1, jnp.int32)
    down = as_column(across)
    mixed = jnp.bitwise_xor(down, jnp.concatenate([across, filler], axis=1))
    repeat = spreader(tiles * LANES)
    wanted = []
    for half in range(groups):
        tags = t_ref[half, t_ref.shape[1] - SUB :, :].astype(jnp.float32).astype(jnp.int32)
        wanted += [tags[:1, TAG + j : TAG + j + 1] for j in range(held)]
    for half in range(groups):
        both = [part(t_ref[q * groups + half].astype(jnp.float32), block) for q in range(cols)]
        for at in range(CORES):
            p = half * CORES + at
            rows = jnp.concatenate([pieces[at] for pieces in both], axis=0)
            spread = jnp.dot(
                rows.astype(jnp.bfloat16), repeat, preferred_element_type=jnp.float32
            )
            spread = jnp.where(mixed == wanted[p], spread, 0.0)
            amp[p * width : (p + 1) * width, :] = spread.astype(jnp.bfloat16)[:, :width]

    for source, base in ((near_ref, 0), (stack, half_steps)):
        if base:
            fetch.wait()

        @pl.loop(0, half_steps)
        def _(g, source=source, base=base):
            here = pl.multiple_of(g * step, step)
            there = pl.multiple_of((base + g) * step, step)
            for k in range(group):
                side[base + g, :, k * width : (k + 1) * width] = source[
                    pl.ds(pl.multiple_of(here + k * width, width), width), :
                ]
            part = lax.dot_general(
                amp[...],
                source[pl.ds(here, step), :],
                (((1,), (1,)), ((), ())),
                preferred_element_type=jnp.float32,
            ).astype(jnp.bfloat16)
            for p in range(pairs):
                for k in range(group):
                    inner[
                        pl.ds(pl.multiple_of(there + k * width, width), width),
                        p * width : (p + 1) * width,
                    ] = part[p * width : (p + 1) * width, k * width : (k + 1) * width]

    for start in range(0, pairs * width, lane_group):
        lanes = slice(start, start + lane_group)
        total = None
        for g in range(2 * half_steps):
            term = jnp.dot(
                side[g], inner[g * step : (g + 1) * step, lanes], preferred_element_type=jnp.float32
            )
            total = term if total is None else total + term
        ladders[:, lanes] = total

    blank = jnp.zeros((width, tiles * LANES - width), jnp.float32)
    for half in range(groups):
        both = []
        for at in range(CORES):
            p = half * CORES + at
            ladder = jnp.concatenate([ladders[:, p * width : (p + 1) * width], blank], axis=1)
            ladder = jnp.where(mixed == wanted[p], ladder, 0.0)
            tall = ladder[:FOLD]
            for start in range(FOLD, width, FOLD):
                tall = tall + ladder[start : start + FOLD]
            tall = jnp.concatenate(
                [tall, jnp.zeros((LANES - FOLD, tiles * LANES), jnp.float32)], axis=0
            )
            flat = fold([ladder[:, t * LANES : (t + 1) * LANES] for t in range(tiles)])
            both.append(flat + tall.T[:width])
        for q in range(cols):
            span = slice(q * block, (q + 1) * block)
            out_ref[q * groups + half] = join(both[0][span], both[1][span]).astype(out_ref.dtype)


def ladder_call(gathered, near, far, labels, cols):
    count, width, _ = near.shape
    pairs = labels.shape[1] - width
    group = 4
    depth, lanes = 2 * count * width, pairs * width
    vmem = pl.BlockSpec(memory_space=pltpu.VMEM)
    anywhere = pl.BlockSpec(memory_space=pl.ANY)
    close = functools.partial(pltpu.with_memory_space_constraint, memory_space=pltpu.VMEM)
    return pl.pallas_call(
        functools.partial(ladder_kernel, cols, group, 2 * LANES),
        out_shape=pltpu.VMEM(gathered.shape, jnp.bfloat16),
        in_specs=[vmem, vmem, anywhere, vmem],
        out_specs=vmem,
        scratch_shapes=[
            pltpu.VMEM((depth, lanes), jnp.bfloat16),
            pltpu.VMEM((lanes, width), jnp.bfloat16),
            pltpu.VMEM((width, lanes), jnp.float32),
            pltpu.VMEM((2 * count // group, width, group * width), jnp.bfloat16),
            pltpu.VMEM((count * width, width), jnp.bfloat16),
            pltpu.SemaphoreType.DMA(()),
        ],
        compiler_params=pltpu.CompilerParams(vmem_limit_bytes=40 * 2**20),
    )(
        close(gathered),
        close(near.reshape(count * width, width)),
        pltpu.with_memory_space_constraint(far.reshape(count * width, width), pltpu.HBM),
        close(labels),
    )


def body(amplitudes, factors, vir_irrep, pair_irrep):
    row_block, pairs_here, col_block = amplitudes.shape
    width = vir_irrep.shape[0]
    rows, cols = width // row_block, width // col_block
    plane = ("col", "pair")
    swap = [(k, k ^ 1) for k in range(rows)]
    labels = jnp.concatenate([vir_irrep, pair_irrep])[None, :]

    other_factors = lax.ppermute(factors, "row", swap)

    allowed, partner, tags = mask_call(labels, width, row_block, pairs_here, col_block)
    sent = spread_call(amplitudes, rows)
    tall = lax.all_to_all(sent, "row", 0, 0, tiled=True)
    groups = cols * lax.axis_size("pair")
    block = fold_call(tall, labels, partner, tags, row_block, col_block, groups)
    gathered = lax.all_to_all(block, plane, 0, 0, tiled=True)
    partial_sums = ladder_call(gathered, other_factors, factors, labels, cols)
    pieces = lax.all_to_all(partial_sums, plane, 0, 0, tiled=True)
    packed = pack_call(pieces, rows, row_block, col_block)
    finals = lax.all_to_all(packed, "row", 0, 0, tiled=True)
    return unpack_call(finals, allowed, amplitudes.shape)


def solution(mesh):
    placed = (P("row", "pair", "col"), P(("row", "col", "pair"), None, None), P(), P("pair"))
    return jax.shard_map(
        body, mesh=mesh, in_specs=placed, out_specs=P("row", "pair", "col"), check_vma=False
    )
```

```python
import functools

import jax
import jax.numpy as jnp
from jax import lax
from jax.experimental import pallas as pl
from jax.experimental.pallas import tpu as pltpu
from jax.sharding import PartitionSpec as P


LANES = 128
FOLD = 80
LEFT = LANES - FOLD
REST = FOLD - LEFT
SUB = 8
TAG = LANES - 2
CORES = 2


def lanes():
    return lax.broadcasted_iota(jnp.int32, (1, LANES), 1)


def turn(x, shift):
    shift = shift % LANES
    return pltpu.roll(x, shift, 1) if shift else x


def join(first, second):
    lane = lanes()
    block = second.shape[0]
    main = jnp.where(lane < FOLD, first, turn(second, FOLD))
    rows, per_row = [], LANES // REST
    for start in range(0, block // SUB, per_row):
        row = jnp.zeros((SUB, LANES), jnp.float32)
        for k in range(min(per_row, block // SUB - start)):
            at = (start + k) * SUB
            moved = turn(second[at : at + SUB], k * REST - LEFT)
            row = jnp.where((lane >= k * REST) & (lane < (k + 1) * REST), moved, row)
        rows.append(row)
    return jnp.concatenate([main] + rows, axis=0)


def joined_rows(block):
    return block + -(-(block // SUB) // (LANES // REST)) * SUB


def part(x, block):
    lane = lanes()
    per_row = LANES // REST
    first = x[:block]
    tail = [
        turn(
            x[block + g // per_row * SUB : block + (g // per_row + 1) * SUB],
            LEFT - g % per_row * REST,
        )
        for g in range(block // SUB)
    ]
    second = jnp.where(lane < LEFT, turn(first, -FOLD), jnp.concatenate(tail, axis=0))
    return first, second


def spreader(columns):
    down = lax.broadcasted_iota(jnp.int32, (LANES, columns), 0)
    across = lax.broadcasted_iota(jnp.int32, (LANES, columns), 1)
    hit = down == across
    for m in range(1, -(-columns // FOLD)):
        hit = hit | (down == across - m * FOLD)
    return jnp.where(hit & (down < FOLD), 1.0, 0.0).astype(jnp.bfloat16)


def fold(pieces):
    lane = lanes()
    total, by_shift = None, {}
    for t, piece in enumerate(pieces):
        base = t * LANES
        for m in range(base // FOLD, -(-(base + LANES) // FOLD)):
            low, high = max(m * FOLD - base, 0), min((m + 1) * FOLD - base, LANES)
            inside = jnp.where((lane >= low) & (lane < high), piece, 0.0)
            shift = (base - m * FOLD) % LANES
            by_shift[shift] = inside if shift not in by_shift else by_shift[shift] + inside
    for shift, piece in by_shift.items():
        moved = turn(piece, shift)
        total = moved if total is None else total + moved
    return total


PACK = 16


def pick(row, index, size):
    out = row[:, :size]
    for k in range(1, row.shape[1] // size):
        out = jnp.where(index == k, row[:, k * size : (k + 1) * size], out)
    return out


def split_labels(label_ref, width):
    return label_ref[:, :width], label_ref[:, width:]


def as_column(row):
    return jnp.broadcast_to(row, (SUB, row.shape[1])).T[:, :1]


def spread_kernel(amp_ref, out_ref):
    row_block, pairs_here, col_block = amp_ref.shape
    held = pairs_here // CORES
    lines = held * col_block
    amp = amp_ref[...].astype(jnp.float32)
    for c in range(CORES):
        lane_side = jnp.concatenate([amp[:, c * held + j, :] for j in range(held)], axis=1)
        column = lane_side.T
        groups = [column[g * PACK : (g + 1) * PACK] for g in range(lines // PACK)]
        rest = LANES - row_block * len(groups)
        groups.append(jnp.zeros((PACK, rest), jnp.float32))
        packed = jnp.concatenate(groups, axis=1).astype(out_ref.dtype)
        for m in range(c, out_ref.shape[0], CORES):
            out_ref[m] = packed


def mask_kernel(width, label_ref, allowed_ref, partner_ref, tag_ref):
    pairs_here, row_block, col_block = allowed_ref.shape
    across, own_pairs = split_labels(label_ref, width)
    held = pairs_here // CORES
    down = as_column(pick(across, lax.axis_index("row"), row_block))
    mine = pick(across, lax.axis_index("col"), col_block)
    for at in range(pairs_here):
        wanted = jnp.bitwise_xor(mine, own_pairs[:, at : at + 1])
        allowed_ref[at] = jnp.where(down == wanted, 1, 0)
    pairs = pick(own_pairs, lax.axis_index("row") % CORES, held)
    partner = as_column(
        jnp.concatenate([jnp.bitwise_xor(mine, pairs[:, j : j + 1]) for j in range(held)], axis=1)
    )
    partner_ref[...] = jnp.broadcast_to(partner, partner_ref.shape)
    lane = lanes()
    tags = jnp.zeros((1, LANES), jnp.float32)
    for j in range(held):
        tags = jnp.where(lane == TAG + j, pairs[:, j : j + 1].astype(jnp.float32), tags)
    tag_ref[...] = jnp.broadcast_to(tags, tag_ref.shape)


def mask_call(labels, width, row_block, pairs_here, col_block):
    vmem = pl.BlockSpec(memory_space=pltpu.VMEM)
    lines = pairs_here // CORES * col_block
    return pl.pallas_call(
        functools.partial(mask_kernel, width),
        out_shape=(
            jax.ShapeDtypeStruct((pairs_here, row_block, col_block), jnp.int32),
            jax.ShapeDtypeStruct((lines, LANES), jnp.int32),
            jax.ShapeDtypeStruct((SUB, LANES), jnp.float32),
        ),
        in_specs=[vmem],
        out_specs=(vmem, vmem, vmem),
        compiler_params=pltpu.CompilerParams(vmem_limit_bytes=8 * 2**20),
    )(pltpu.with_memory_space_constraint(labels, pltpu.VMEM))


def fold_kernel(row_block, col_block, tall_ref, label_ref, partner_ref, tag_ref, out_ref):
    width = tall_ref.shape[0] * row_block
    across, _ = split_labels(label_ref, width)
    lines = partner_ref.shape[0]
    partner = partner_ref[...]
    lane = lanes()
    filler = jnp.full((1, LANES - FOLD), -1, jnp.int32)
    folded = [jnp.zeros((PACK, LANES), jnp.float32) for _ in range(lines // PACK)]
    for m in range(width // FOLD):
        labels = jnp.concatenate([across[:, m * FOLD : (m + 1) * FOLD], filler], axis=1)
        for k in range(FOLD // row_block):
            low = k * row_block
            here = jnp.where((lane >= low) & (lane < low + row_block), labels, -1)
            piece = tall_ref[m * (FOLD // row_block) + k].astype(jnp.float32)
            for g in range(lines // PACK):
                fits = partner[g * PACK : (g + 1) * PACK] == here
                folded[g] = folded[g] + jnp.where(fits, turn(piece, (k - g) * row_block), 0.0)
    block = jnp.concatenate(folded, axis=0)
    block = join(block[:col_block], block[col_block:])
    block = jnp.concatenate([block[:-SUB], block[-SUB:] + tag_ref[...]], axis=0)
    block = block.astype(out_ref.dtype)
    for m in range(out_ref.shape[0]):
        out_ref[m] = block


def spread_call(amplitudes, rows):
    vmem = pl.BlockSpec(memory_space=pltpu.VMEM)
    return pl.pallas_call(
        spread_kernel,
        out_shape=jax.ShapeDtypeStruct((rows, PACK, LANES), amplitudes.dtype),
        in_specs=[vmem],
        out_specs=vmem,
        compiler_params=pltpu.CompilerParams(vmem_limit_bytes=8 * 2**20),
    )(pltpu.with_memory_space_constraint(amplitudes, pltpu.HBM))


def fold_call(tall, labels, partner, tags, row_block, col_block, groups):
    vmem = pl.BlockSpec(memory_space=pltpu.VMEM)
    close = functools.partial(pltpu.with_memory_space_constraint, memory_space=pltpu.VMEM)
    return pl.pallas_call(
        functools.partial(fold_kernel, row_block, col_block),
        out_shape=jax.ShapeDtypeStruct((groups, joined_rows(col_block), LANES), tall.dtype),
        in_specs=[vmem] * 4,
        out_specs=vmem,
        compiler_params=pltpu.CompilerParams(vmem_limit_bytes=8 * 2**20),
    )(close(tall), close(labels), close(partner), close(tags))


def pack_kernel(row_block, col_block, pieces_ref, out_ref):
    total = pieces_ref[0].astype(jnp.float32)
    for m in range(1, pieces_ref.shape[0]):
        total = total + pieces_ref[m].astype(jnp.float32)
    total = jnp.concatenate(part(total, col_block), axis=0)
    lane = lanes()
    period = FOLD // row_block
    for k in range(period):
        packed = jnp.zeros((PACK, LANES), jnp.float32)
        for g in range(total.shape[0] // PACK):
            moved = turn(total[g * PACK : (g + 1) * PACK], (g - k) * row_block)
            packed = jnp.where(
                (lane >= g * row_block) & (lane < (g + 1) * row_block), moved, packed
            )
        for r in range(k, out_ref.shape[0], period):
            out_ref[r] = packed


def unpack_kernel(finals_ref, allowed_ref, out_ref):
    row_block, pairs_here, col_block = out_ref.shape
    held = pairs_here // CORES
    lines = held * col_block
    for c in range(CORES):
        total = finals_ref[c]
        for z in range(CORES + c, finals_ref.shape[0], CORES):
            total = total + finals_ref[z]
        spread = jnp.concatenate(
            [
                turn(total, -g * row_block)
                for g in range(lines // PACK)
            ],
            axis=0,
        )
        spread = spread.T[:row_block]
        for j in range(held):
            at = c * held + j
            piece = spread[:, j * col_block : (j + 1) * col_block]
            out_ref[:, at, :] = jnp.where(allowed_ref[at] != 0, piece, 0.0)


def pack_call(pieces, rows, row_block, col_block):
    close = functools.partial(pltpu.with_memory_space_constraint, memory_space=pltpu.VMEM)
    vmem = pl.BlockSpec(memory_space=pltpu.VMEM)
    return pl.pallas_call(
        functools.partial(pack_kernel, row_block, col_block),
        out_shape=jax.ShapeDtypeStruct((rows, PACK, LANES), jnp.float32),
        in_specs=[vmem],
        out_specs=vmem,
        compiler_params=pltpu.CompilerParams(vmem_limit_bytes=8 * 2**20),
    )(close(pieces))


def unpack_call(finals, allowed, shape):
    close = functools.partial(pltpu.with_memory_space_constraint, memory_space=pltpu.VMEM)
    vmem = pl.BlockSpec(memory_space=pltpu.VMEM)
    return pl.pallas_call(
        unpack_kernel,
        out_shape=jax.ShapeDtypeStruct(shape, jnp.float32),
        in_specs=[vmem] * 2,
        out_specs=vmem,
        compiler_params=pltpu.CompilerParams(vmem_limit_bytes=8 * 2**20),
    )(close(finals), close(allowed))


def ladder_kernel(
    cols,
    group,
    lane_group,
    t_ref,
    near_ref,
    far_ref,
    label_ref,
    out_ref,
    inner,
    amp,
    ladders,
    side,
    stack,
    arrived,
):
    half_depth, width = near_ref.shape
    across, own_pairs = split_labels(label_ref, width)
    groups = t_ref.shape[0] // cols
    held = own_pairs.shape[1] // CORES
    pairs = held * groups
    tiles = -(-width // LANES)
    block = width // cols
    step = group * width
    half_steps = half_depth // step

    fetch = pltpu.make_async_copy(far_ref, stack, arrived)
    fetch.start()
    filler = jnp.full((1, tiles * LANES - width), -1, jnp.int32)
    down = as_column(across)
    mixed = jnp.bitwise_xor(down, jnp.concatenate([across, filler], axis=1))
    repeat = spreader(tiles * LANES)
    wanted = []
    for half in range(groups):
        tags = t_ref[half, t_ref.shape[1] - SUB :, :].astype(jnp.float32).astype(jnp.int32)
        wanted += [tags[:1, TAG + j : TAG + j + 1] for j in range(held)]
    for half in range(groups):
        both = [part(t_ref[q * groups + half].astype(jnp.float32), block) for q in range(cols)]
        for at in range(CORES):
            p = half * CORES + at
            rows = jnp.concatenate([pieces[at] for pieces in both], axis=0)
            spread = jnp.dot(
                rows.astype(jnp.bfloat16), repeat, preferred_element_type=jnp.float32
            )
            spread = jnp.where(mixed == wanted[p], spread, 0.0)
            amp[p * width : (p + 1) * width, :] = spread.astype(jnp.bfloat16)[:, :width]

    for source, base in ((near_ref, 0), (stack, half_steps)):
        if base:
            fetch.wait()

        for g in range(half_steps):
            here, there = g * step, (base + g) * step
            side[:, there : there + step] = jnp.concatenate(
                [
                    source[here + k * width : here + (k + 1) * width, :]
                    for k in range(group)
                ],
                axis=1,
            )
            product = lax.dot_general(
                amp[...],
                source[here : here + step, :],
                (((1,), (1,)), ((), ())),
                preferred_element_type=jnp.float32,
            ).astype(jnp.bfloat16)
            for p in range(pairs):
                for k in range(group):
                    inner[
                        there + k * width : there + (k + 1) * width,
                        p * width : (p + 1) * width,
                    ] = product[p * width : (p + 1) * width, k * width : (k + 1) * width]

    for start in range(0, pairs * width, lane_group):
        columns = slice(start, start + lane_group)
        ladders[:, columns] = jnp.dot(
            side[...], inner[:, columns], preferred_element_type=jnp.float32
        )

    blank = jnp.zeros((width, tiles * LANES - width), jnp.float32)
    for half in range(groups):
        both = []
        for at in range(CORES):
            p = half * CORES + at
            ladder = jnp.concatenate([ladders[:, p * width : (p + 1) * width], blank], axis=1)
            ladder = jnp.where(mixed == wanted[p], ladder, 0.0)
            tall = ladder[:FOLD]
            for start in range(FOLD, width, FOLD):
                tall = tall + ladder[start : start + FOLD]
            tall = jnp.concatenate(
                [tall, jnp.zeros((LANES - FOLD, tiles * LANES), jnp.float32)], axis=0
            )
            flat = fold([ladder[:, t * LANES : (t + 1) * LANES] for t in range(tiles)])
            both.append(flat + tall.T[:width])
        for q in range(cols):
            span = slice(q * block, (q + 1) * block)
            out_ref[q * groups + half] = join(both[0][span], both[1][span]).astype(out_ref.dtype)


def ladder_call(gathered, near, far, labels, cols):
    count, width, _ = near.shape
    pairs = labels.shape[1] - width
    group = 4
    depth, lanes = 2 * count * width, pairs * width
    vmem = pl.BlockSpec(memory_space=pltpu.VMEM)
    anywhere = pl.BlockSpec(memory_space=pl.ANY)
    close = functools.partial(pltpu.with_memory_space_constraint, memory_space=pltpu.VMEM)
    return pl.pallas_call(
        functools.partial(ladder_kernel, cols, group, 2 * LANES),
        out_shape=pltpu.VMEM(gathered.shape, jnp.bfloat16),
        in_specs=[vmem, vmem, anywhere, vmem],
        out_specs=vmem,
        scratch_shapes=[
            pltpu.VMEM((depth, lanes), jnp.bfloat16),
            pltpu.VMEM((lanes, width), jnp.bfloat16),
            pltpu.VMEM((width, lanes), jnp.float32),
            pltpu.VMEM((width, depth), jnp.bfloat16),
            pltpu.VMEM((count * width, width), jnp.bfloat16),
            pltpu.SemaphoreType.DMA(()),
        ],
        compiler_params=pltpu.CompilerParams(vmem_limit_bytes=40 * 2**20),
    )(
        close(gathered),
        close(near.reshape(count * width, width)),
        pltpu.with_memory_space_constraint(far.reshape(count * width, width), pltpu.HBM),
        close(labels),
    )


def body(amplitudes, factors, vir_irrep, pair_irrep):
    row_block, pairs_here, col_block = amplitudes.shape
    width = vir_irrep.shape[0]
    rows, cols = width // row_block, width // col_block
    plane = ("col", "pair")
    swap = [(k, k ^ 1) for k in range(rows)]
    labels = jnp.concatenate([vir_irrep, pair_irrep])[None, :]

    other_factors = lax.ppermute(factors, "row", swap)

    allowed, partner, tags = mask_call(labels, width, row_block, pairs_here, col_block)
    sent = spread_call(amplitudes, rows)
    tall = lax.all_to_all(sent, "row", 0, 0, tiled=True)
    groups = cols * lax.axis_size("pair")
    block = fold_call(tall, labels, partner, tags, row_block, col_block, groups)
    gathered = lax.all_to_all(block, plane, 0, 0, tiled=True)
    partial_sums = ladder_call(gathered, other_factors, factors, labels, cols)
    pieces = lax.all_to_all(partial_sums, plane, 0, 0, tiled=True)
    packed = pack_call(pieces, rows, row_block, col_block)
    finals = lax.all_to_all(packed, "row", 0, 0, tiled=True)
    return unpack_call(finals, allowed, amplitudes.shape)


def solution(mesh):
    placed = (P("row", "pair", "col"), P(("row", "col", "pair"), None, None), P(), P("pair"))
    return jax.shard_map(
        body, mesh=mesh, in_specs=placed, out_specs=P("row", "pair", "col"), check_vma=False
    )
```

```python
import functools

import jax
import jax.numpy as jnp
from jax import lax
from jax.experimental import pallas as pl
from jax.experimental.pallas import tpu as pltpu
from jax.sharding import PartitionSpec as P


LANES = 128
FOLD = 80
LEFT = LANES - FOLD
REST = FOLD - LEFT
SUB = 8
TAG = LANES - 2
CORES = 2


def lanes():
    return lax.broadcasted_iota(jnp.int32, (1, LANES), 1)


def turn(x, shift):
    shift = shift % LANES
    return pltpu.roll(x, shift, 1) if shift else x


def join(first, second):
    lane = lanes()
    block = second.shape[0]
    main = jnp.where(lane < FOLD, first, turn(second, FOLD))
    rows, per_row = [], LANES // REST
    for start in range(0, block // SUB, per_row):
        row = jnp.zeros((SUB, LANES), jnp.float32)
        for k in range(min(per_row, block // SUB - start)):
            at = (start + k) * SUB
            moved = turn(second[at : at + SUB], k * REST - LEFT)
            row = jnp.where((lane >= k * REST) & (lane < (k + 1) * REST), moved, row)
        rows.append(row)
    return jnp.concatenate([main] + rows, axis=0)


def joined_rows(block):
    return block + -(-(block // SUB) // (LANES // REST)) * SUB


def part(x, block):
    lane = lanes()
    per_row = LANES // REST
    first = x[:block]
    tail = [
        turn(
            x[block + g // per_row * SUB : block + (g // per_row + 1) * SUB],
            LEFT - g % per_row * REST,
        )
        for g in range(block // SUB)
    ]
    second = jnp.where(lane < LEFT, turn(first, -FOLD), jnp.concatenate(tail, axis=0))
    return first, second


def spreader(columns):
    down = lax.broadcasted_iota(jnp.int32, (LANES, columns), 0)
    across = lax.broadcasted_iota(jnp.int32, (LANES, columns), 1)
    hit = down == across
    for m in range(1, -(-columns // FOLD)):
        hit = hit | (down == across - m * FOLD)
    return jnp.where(hit & (down < FOLD), 1.0, 0.0).astype(jnp.bfloat16)


def fold(pieces):
    lane = lanes()
    total, by_shift = None, {}
    for t, piece in enumerate(pieces):
        base = t * LANES
        for m in range(base // FOLD, -(-(base + LANES) // FOLD)):
            low, high = max(m * FOLD - base, 0), min((m + 1) * FOLD - base, LANES)
            inside = jnp.where((lane >= low) & (lane < high), piece, 0.0)
            shift = (base - m * FOLD) % LANES
            by_shift[shift] = inside if shift not in by_shift else by_shift[shift] + inside
    for shift, piece in by_shift.items():
        moved = turn(piece, shift)
        total = moved if total is None else total + moved
    return total


PACK = 16


def pick(row, index, size):
    out = row[:, :size]
    for k in range(1, row.shape[1] // size):
        out = jnp.where(index == k, row[:, k * size : (k + 1) * size], out)
    return out


def split_labels(label_ref, width):
    return label_ref[:, :width], label_ref[:, width:]


def as_column(row):
    return jnp.broadcast_to(row, (SUB, row.shape[1])).T[:, :1]


def spread_kernel(amp_ref, out_ref):
    row_block, pairs_here, col_block = amp_ref.shape
    held = pairs_here // CORES
    lines = held * col_block
    amp = amp_ref[...].astype(jnp.float32)
    for c in range(CORES):
        lane_side = jnp.concatenate([amp[:, c * held + j, :] for j in range(held)], axis=1)
        column = lane_side.T
        groups = [column[g * PACK : (g + 1) * PACK] for g in range(lines // PACK)]
        rest = LANES - row_block * len(groups)
        groups.append(jnp.zeros((PACK, rest), jnp.float32))
        packed = jnp.concatenate(groups, axis=1).astype(out_ref.dtype)
        for m in range(c, out_ref.shape[0], CORES):
            out_ref[m] = packed


def mask_kernel(width, label_ref, allowed_ref, partner_ref, tag_ref):
    pairs_here, row_block, col_block = allowed_ref.shape
    across, own_pairs = split_labels(label_ref, width)
    held = pairs_here // CORES
    down = as_column(pick(across, lax.axis_index("row"), row_block))
    mine = pick(across, lax.axis_index("col"), col_block)
    for at in range(pairs_here):
        wanted = jnp.bitwise_xor(mine, own_pairs[:, at : at + 1])
        allowed_ref[at] = jnp.where(down == wanted, 1, 0)
    pairs = pick(own_pairs, lax.axis_index("row") % CORES, held)
    partner = as_column(
        jnp.concatenate([jnp.bitwise_xor(mine, pairs[:, j : j + 1]) for j in range(held)], axis=1)
    )
    partner_ref[...] = jnp.broadcast_to(partner, partner_ref.shape)
    lane = lanes()
    tags = jnp.zeros((1, LANES), jnp.float32)
    for j in range(held):
        tags = jnp.where(lane == TAG + j, pairs[:, j : j + 1].astype(jnp.float32), tags)
    tag_ref[...] = jnp.broadcast_to(tags, tag_ref.shape)


def mask_call(labels, width, row_block, pairs_here, col_block):
    vmem = pl.BlockSpec(memory_space=pltpu.VMEM)
    lines = pairs_here // CORES * col_block
    return pl.pallas_call(
        functools.partial(mask_kernel, width),
        out_shape=(
            jax.ShapeDtypeStruct((pairs_here, row_block, col_block), jnp.int32),
            jax.ShapeDtypeStruct((lines, LANES), jnp.int32),
            jax.ShapeDtypeStruct((SUB, LANES), jnp.float32),
        ),
        in_specs=[vmem],
        out_specs=(vmem, vmem, vmem),
        compiler_params=pltpu.CompilerParams(vmem_limit_bytes=8 * 2**20),
    )(pltpu.with_memory_space_constraint(labels, pltpu.VMEM))


def fold_kernel(row_block, col_block, tall_ref, label_ref, partner_ref, tag_ref, out_ref):
    width = tall_ref.shape[0] * row_block
    across, _ = split_labels(label_ref, width)
    lines = partner_ref.shape[0]
    partner = partner_ref[...]
    lane = lanes()
    filler = jnp.full((1, LANES - FOLD), -1, jnp.int32)
    folded = [jnp.zeros((PACK, LANES), jnp.float32) for _ in range(lines // PACK)]
    for m in range(width // FOLD):
        labels = jnp.concatenate([across[:, m * FOLD : (m + 1) * FOLD], filler], axis=1)
        for k in range(FOLD // row_block):
            low = k * row_block
            here = jnp.where((lane >= low) & (lane < low + row_block), labels, -1)
            piece = tall_ref[m * (FOLD // row_block) + k].astype(jnp.float32)
            for g in range(lines // PACK):
                fits = partner[g * PACK : (g + 1) * PACK] == here
                folded[g] = folded[g] + jnp.where(fits, turn(piece, (k - g) * row_block), 0.0)
    block = jnp.concatenate(folded, axis=0)
    block = join(block[:col_block], block[col_block:])
    block = jnp.concatenate([block[:-SUB], block[-SUB:] + tag_ref[...]], axis=0)
    block = block.astype(out_ref.dtype)
    for m in range(out_ref.shape[0]):
        out_ref[m] = block


def spread_call(amplitudes, rows):
    vmem = pl.BlockSpec(memory_space=pltpu.VMEM)
    return pl.pallas_call(
        spread_kernel,
        out_shape=jax.ShapeDtypeStruct((rows, PACK, LANES), amplitudes.dtype),
        in_specs=[vmem],
        out_specs=vmem,
        compiler_params=pltpu.CompilerParams(vmem_limit_bytes=8 * 2**20),
    )(pltpu.with_memory_space_constraint(amplitudes, pltpu.HBM))


def fold_call(tall, labels, partner, tags, row_block, col_block, groups):
    vmem = pl.BlockSpec(memory_space=pltpu.VMEM)
    close = functools.partial(pltpu.with_memory_space_constraint, memory_space=pltpu.VMEM)
    return pl.pallas_call(
        functools.partial(fold_kernel, row_block, col_block),
        out_shape=jax.ShapeDtypeStruct((groups, joined_rows(col_block), LANES), tall.dtype),
        in_specs=[vmem] * 4,
        out_specs=vmem,
        compiler_params=pltpu.CompilerParams(vmem_limit_bytes=8 * 2**20),
    )(close(tall), close(labels), close(partner), close(tags))


def pack_kernel(row_block, col_block, pieces_ref, out_ref):
    total = pieces_ref[0].astype(jnp.float32)
    for m in range(1, pieces_ref.shape[0]):
        total = total + pieces_ref[m].astype(jnp.float32)
    total = jnp.concatenate(part(total, col_block), axis=0)
    lane = lanes()
    period = FOLD // row_block
    for k in range(period):
        packed = jnp.zeros((PACK, LANES), jnp.float32)
        for g in range(total.shape[0] // PACK):
            moved = turn(total[g * PACK : (g + 1) * PACK], (g - k) * row_block)
            packed = jnp.where(
                (lane >= g * row_block) & (lane < (g + 1) * row_block), moved, packed
            )
        for r in range(k, out_ref.shape[0], period):
            out_ref[r] = packed


def unpack_kernel(finals_ref, allowed_ref, out_ref):
    row_block, pairs_here, col_block = out_ref.shape
    held = pairs_here // CORES
    lines = held * col_block
    for c in range(CORES):
        total = finals_ref[c]
        for z in range(CORES + c, finals_ref.shape[0], CORES):
            total = total + finals_ref[z]
        spread = jnp.concatenate(
            [
                turn(total, -g * row_block)
                for g in range(lines // PACK)
            ],
            axis=0,
        )
        spread = spread.T[:row_block]
        for j in range(held):
            at = c * held + j
            piece = spread[:, j * col_block : (j + 1) * col_block]
            out_ref[:, at, :] = jnp.where(allowed_ref[at] != 0, piece, 0.0)


def pack_call(pieces, rows, row_block, col_block):
    close = functools.partial(pltpu.with_memory_space_constraint, memory_space=pltpu.VMEM)
    vmem = pl.BlockSpec(memory_space=pltpu.VMEM)
    return pl.pallas_call(
        functools.partial(pack_kernel, row_block, col_block),
        out_shape=jax.ShapeDtypeStruct((rows, PACK, LANES), jnp.float32),
        in_specs=[vmem],
        out_specs=vmem,
        compiler_params=pltpu.CompilerParams(vmem_limit_bytes=8 * 2**20),
    )(close(pieces))


def unpack_call(finals, allowed, shape):
    close = functools.partial(pltpu.with_memory_space_constraint, memory_space=pltpu.VMEM)
    vmem = pl.BlockSpec(memory_space=pltpu.VMEM)
    return pl.pallas_call(
        unpack_kernel,
        out_shape=jax.ShapeDtypeStruct(shape, jnp.float32),
        in_specs=[vmem] * 2,
        out_specs=vmem,
        compiler_params=pltpu.CompilerParams(vmem_limit_bytes=8 * 2**20),
    )(close(finals), close(allowed))


def ladder_kernel(
    cols,
    group,
    lane_group,
    t_ref,
    near_ref,
    far_ref,
    label_ref,
    out_ref,
    inner,
    amp,
    ladders,
    side,
    stack,
    arrived,
):
    half_depth, width = near_ref.shape
    across, own_pairs = split_labels(label_ref, width)
    groups = t_ref.shape[0] // cols
    held = own_pairs.shape[1] // CORES
    pairs = held * groups
    tiles = -(-width // LANES)
    block = width // cols
    step = group * width
    half_steps = half_depth // step

    fetch = pltpu.make_async_copy(far_ref, stack, arrived)
    fetch.start()
    filler = jnp.full((1, tiles * LANES - width), -1, jnp.int32)
    down = as_column(across)
    mixed = jnp.bitwise_xor(down, jnp.concatenate([across, filler], axis=1))
    repeat = spreader(tiles * LANES)
    wanted = []
    for half in range(groups):
        tags = t_ref[half, t_ref.shape[1] - SUB :, :].astype(jnp.float32).astype(jnp.int32)
        wanted += [tags[:1, TAG + j : TAG + j + 1] for j in range(held)]
    for half in range(groups):
        both = [part(t_ref[q * groups + half].astype(jnp.float32), block) for q in range(cols)]
        for at in range(CORES):
            p = half * CORES + at
            rows = jnp.concatenate([pieces[at] for pieces in both], axis=0)
            spread = jnp.dot(
                rows.astype(jnp.bfloat16), repeat, preferred_element_type=jnp.float32
            )
            spread = jnp.where(mixed == wanted[p], spread, 0.0)
            amp[p * width : (p + 1) * width, :] = spread.astype(jnp.bfloat16)[:, :width]

    for source, base in ((near_ref, 0), (stack, half_steps)):
        if base:
            fetch.wait()

        for g in range(half_steps):
            here, there = g * step, (base + g) * step
            side[:, there : there + step] = jnp.concatenate(
                [
                    source[here + k * width : here + (k + 1) * width, :]
                    for k in range(group)
                ],
                axis=1,
            )
            product = lax.dot_general(
                amp[...],
                source[here : here + step, :],
                (((1,), (1,)), ((), ())),
                preferred_element_type=jnp.float32,
            ).astype(jnp.bfloat16)
            for p in range(pairs):
                for k in range(group):
                    inner[
                        there + k * width : there + (k + 1) * width,
                        p * width : (p + 1) * width,
                    ] = product[p * width : (p + 1) * width, k * width : (k + 1) * width]

    blank = jnp.zeros((width, tiles * LANES - width), jnp.float32)

    def finish(half):
        both = []
        for at in range(CORES):
            p = half * CORES + at
            ladder = jnp.concatenate([ladders[:, p * width : (p + 1) * width], blank], axis=1)
            ladder = jnp.where(mixed == wanted[p], ladder, 0.0)
            tall = ladder[:FOLD]
            for start in range(FOLD, width, FOLD):
                tall = tall + ladder[start : start + FOLD]
            tall = jnp.concatenate(
                [tall, jnp.zeros((LANES - FOLD, tiles * LANES), jnp.float32)], axis=0
            )
            flat = fold([ladder[:, t * LANES : (t + 1) * LANES] for t in range(tiles)])
            both.append(flat + tall.T[:width])
        for q in range(cols):
            span = slice(q * block, (q + 1) * block)
            out_ref[q * groups + half] = join(both[0][span], both[1][span]).astype(out_ref.dtype)

    done = 0
    for start in range(0, pairs * width, lane_group):
        columns = slice(start, start + lane_group)
        ladders[:, columns] = jnp.dot(
            side[...], inner[:, columns], preferred_element_type=jnp.float32
        )
        while (done + 1) * held * width <= start + lane_group:
            finish(done)
            done += 1


def ladder_call(gathered, near, far, labels, cols):
    count, width, _ = near.shape
    pairs = labels.shape[1] - width
    group = 4
    depth, lanes = 2 * count * width, pairs * width
    vmem = pl.BlockSpec(memory_space=pltpu.VMEM)
    anywhere = pl.BlockSpec(memory_space=pl.ANY)
    close = functools.partial(pltpu.with_memory_space_constraint, memory_space=pltpu.VMEM)
    return pl.pallas_call(
        functools.partial(ladder_kernel, cols, group, 2 * LANES),
        out_shape=pltpu.VMEM(gathered.shape, jnp.bfloat16),
        in_specs=[vmem, vmem, anywhere, vmem],
        out_specs=vmem,
        scratch_shapes=[
            pltpu.VMEM((depth, lanes), jnp.bfloat16),
            pltpu.VMEM((lanes, width), jnp.bfloat16),
            pltpu.VMEM((width, lanes), jnp.float32),
            pltpu.VMEM((width, depth), jnp.bfloat16),
            pltpu.VMEM((count * width, width), jnp.bfloat16),
            pltpu.SemaphoreType.DMA(()),
        ],
        compiler_params=pltpu.CompilerParams(vmem_limit_bytes=40 * 2**20),
    )(
        close(gathered),
        close(near.reshape(count * width, width)),
        pltpu.with_memory_space_constraint(far.reshape(count * width, width), pltpu.HBM),
        close(labels),
    )


def body(amplitudes, factors, vir_irrep, pair_irrep):
    row_block, pairs_here, col_block = amplitudes.shape
    width = vir_irrep.shape[0]
    rows, cols = width // row_block, width // col_block
    plane = ("col", "pair")
    swap = [(k, k ^ 1) for k in range(rows)]
    labels = jnp.concatenate([vir_irrep, pair_irrep])[None, :]

    other_factors = lax.ppermute(factors, "row", swap)

    allowed, partner, tags = mask_call(labels, width, row_block, pairs_here, col_block)
    sent = spread_call(amplitudes, rows)
    tall = lax.all_to_all(sent, "row", 0, 0, tiled=True)
    groups = cols * lax.axis_size("pair")
    block = fold_call(tall, labels, partner, tags, row_block, col_block, groups)
    gathered = lax.all_to_all(block, plane, 0, 0, tiled=True)
    partial_sums = ladder_call(gathered, other_factors, factors, labels, cols)
    pieces = lax.all_to_all(partial_sums, plane, 0, 0, tiled=True)
    packed = pack_call(pieces, rows, row_block, col_block)
    finals = lax.all_to_all(packed, "row", 0, 0, tiled=True)
    return unpack_call(finals, allowed, amplitudes.shape)


def solution(mesh):
    placed = (P("row", "pair", "col"), P(("row", "col", "pair"), None, None), P(), P("pair"))
    return jax.shard_map(
        body, mesh=mesh, in_specs=placed, out_specs=P("row", "pair", "col"), check_vma=False
    )
```
